32 devices in a mesh: ray: 4 (over x, core), vox: 8 (over z, y).
Axes of the slice: x: 2, y: 2, z: 4, core: 2. Of those that a mesh axis runs over, the one named last changes fastest.
Arguments:
- tiles: float32 [2048, 128, 128], P(('ray', 'vox')), may hold values from -0.25 to 0.25
- tile_ray: int32 [2048], P(('ray', 'vox')), may hold values from 0 to 15
- tile_vox: int32 [2048], P(('ray', 'vox')), may hold values from 0 to 511, as said below
- tile_count: int32 [32], P(('ray', 'vox')), may hold values from 1 to 64, as said below
- travel: float32 [512, 128], P(('ray', 'vox')), may hold values from -6 to 6
Outputs:
- solution: float32 [512, 128], P('vox')
- direction: float32 [512, 128], P('vox')
The draws below stay inside these ranges and needn't reach their ends.
Inputs may be any that keep to these rules, and one draw needn't show every extreme that they name: `tile_count`: each entry is 1 to 64; some device has exactly 64 live slots. Among the 64 slots of one device (live or not), at most 16 have voxel blocks in the same range of 64 blocks (same tile_vox // 64); on every device some range is named by exactly 16 slots.
All inputs are finite; a program needn't handle non-finite values.
Results may differ from the reference program's by a relative error of at most 0.00017.
Values sent between devices are 32-bit elements; how exact they have to be, the bound alone decides.
No kernel may reach another device: no remote copies, remote signals or barrier semaphores. Data moves between devices by JAX's collectives and lax.ppermute only.
A program may use at most 64 MiB of HBM per device.

```python
import jax
import jax.numpy as jnp
import numpy as np
from jax import lax

BLK = 128
RB_DEV = 16
TILES_DEV = 64
VBD = 64
ITERS = 2
NRB = 512
TILES = 2048
VB = 512
CAP = 16
N_VOX = 8
DEVICES = 32


def draw_tile_count(key, part):
    key_shift = jax.random.fold_in(key, 11)
    key_jitter = jax.random.fold_in(key, 12)
    key_pick = jax.random.fold_in(key, 13)
    divisors = jnp.array(np.array([1, 2, 4, 8], dtype=np.int32))
    level = jax.random.randint(key_shift, (DEVICES,), 0, 4)
    base = TILES_DEV // divisors[level]
    jitter = jax.random.randint(key_jitter, (DEVICES,), 0, TILES_DEV) % (base // 2 + 1)
    counts = jnp.maximum(base - jitter, 1)
    chosen = jax.random.randint(key_pick, (), 0, DEVICES)
    counts = jnp.where(jnp.arange(DEVICES) == chosen, TILES_DEV, counts)
    return counts.astype(jnp.int32)


def draw_tile_vox(key, part):
    device_keys = jax.random.split(jax.random.fold_in(key, 21), DEVICES)
    slot_index = jnp.arange(TILES_DEV, dtype=jnp.int32)
    group_index = jnp.where(slot_index < CAP, 0, 1 + (slot_index - CAP) % (N_VOX - 1))

    def one_device(device_key):
        key_perm = jax.random.fold_in(device_key, 1)
        key_order = jax.random.fold_in(device_key, 2)
        key_local = jax.random.fold_in(device_key, 3)
        owners = jax.random.permutation(key_perm, N_VOX)[group_index]
        owners = owners[jax.random.permutation(key_order, TILES_DEV)]
        local_block = jax.random.randint(key_local, (TILES_DEV,), 0, VBD)
        return owners * VBD + local_block
    return jax.vmap(one_device)(device_keys).reshape(TILES).astype(jnp.int32)


def touch_ends(entries, stream_key, smallest, top_value):
    spot = [jax.random.randint(jax.random.fold_in(stream_key, axis), (), 0, length) for axis, length in enumerate(entries.shape)]
    longest = entries.shape.index(max(entries.shape))
    neighbour = spot[:longest] + [(spot[longest] + 1) % entries.shape[longest]] + spot[longest + 1:]
    return entries.at[tuple(spot)].set(smallest).at[tuple(neighbour)].set(top_value)


def block_scale(own_key, extent, shards, low, high):
    factor_of = 1.0
    for axis_at, blocks in shards:
        heights = jax.random.uniform(jax.random.fold_in(jax.random.fold_in(own_key, 6), axis_at), (blocks,), jnp.float32, low / len(shards), high / len(shards))
        factor_of = factor_of * jnp.repeat(jnp.exp(heights), extent[axis_at] // blocks).reshape((-1,) + (1,) * (len(extent) - 1 - axis_at))
    return factor_of


def normal_values(stream_key, extent, deviation, most, cuts=(), kind=jnp.bfloat16):
    drawn = jax.random.normal(stream_key, extent, jnp.float32) * deviation
    if len(cuts) > 0:
        drawn = block_scale(stream_key, extent, cuts, -0.22, 0.18) * drawn
    return jnp.clip(drawn, min=-most, max=most).astype(kind)


def setup_inputs(seed: int = 0) -> dict:
    splits = jax.random.split(jax.random.key(seed), 6)
    tiles = normal_values(splits[0], (TILES, BLK, BLK), (BLK * 4) ** -0.5, 0.25, ((0, 32),), jnp.float32)
    tile_ray = touch_ends(jax.random.randint(splits[1], (TILES,), 0, RB_DEV), jax.random.fold_in(splits[1], 1), 0, RB_DEV - 1).astype(jnp.int32)
    tile_vox = draw_tile_vox(jax.random.fold_in(splits[5], 71), 0)
    tile_count = draw_tile_count(jax.random.fold_in(splits[5], 71), 0)
    travel = normal_values(splits[4], (NRB, BLK), 1.0, 6.0, ((0, 32),), jnp.float32)
    return dict(tiles=tiles, tile_ray=tile_ray, tile_vox=tile_vox, tile_count=tile_count, travel=travel)


HIGH = lax.Precision.HIGHEST

def reference(tiles, tile_ray, tile_vox, tile_count, travel):
    index_all = jnp.arange(TILES, dtype=jnp.int32)
    owner = (index_all // TILES_DEV).astype(jnp.int32)
    ray_rows = (owner * RB_DEV + tile_ray).astype(jnp.int32)
    live = (index_all % TILES_DEV < tile_count[owner]).astype(jnp.float32)[:, None]

    def forward(vox_vec):
        prod = jnp.einsum('tij,tj->ti', tiles, vox_vec[tile_vox], precision=HIGH) * live
        return jax.ops.segment_sum(prod, ray_rows, num_segments=NRB)

    def backward(ray_vec):
        prod = jnp.einsum('tij,ti->tj', tiles, ray_vec[ray_rows], precision=HIGH) * live
        return jax.ops.segment_sum(prod, tile_vox, num_segments=VB)
    beta_now = jnp.sqrt(jnp.sum(travel * travel))
    ray_vec = travel / beta_now
    vox_vec = backward(ray_vec)
    alpha_now = jnp.sqrt(jnp.sum(vox_vec * vox_vec))
    vox_vec = vox_vec / alpha_now
    direction = vox_vec
    solution = jnp.zeros_like(vox_vec)
    phibar = beta_now
    rhobar = alpha_now
    for step in range(ITERS):
        ray_vec = forward(vox_vec) - alpha_now * ray_vec
        beta_now = jnp.sqrt(jnp.sum(ray_vec * ray_vec))
        ray_vec = ray_vec / beta_now
        vox_vec = backward(ray_vec) - beta_now * vox_vec
        alpha_now = jnp.sqrt(jnp.sum(vox_vec * vox_vec))
        vox_vec = vox_vec / alpha_now
        rho_val = jnp.sqrt(rhobar * rhobar + beta_now * beta_now)
        cosine = rhobar / rho_val
        sine_val = beta_now / rho_val
        theta_val = sine_val * alpha_now
        rhobar = -cosine * alpha_now
        phi_val = cosine * phibar
        phibar = sine_val * phibar
        solution = solution + phi_val / rho_val * direction
        direction = vox_vec - theta_val / rho_val * direction
    return (solution, direction)
```

```python
import functools

import jax
import jax.numpy as jnp
from jax import lax
from jax.experimental import pallas as pl
from jax.experimental.pallas import tpu as pltpu
from jax.sharding import PartitionSpec as P

VBD = 64
LANES = 128
GROUP = 8
F32 = jnp.float32
BF16 = jnp.bfloat16


class Sizes:
    def __init__(self, n_ray, n_vox, slots, ray_blocks):
        self.n_ray, self.n_vox, self.slots, self.ray_blocks = n_ray, n_vox, slots, ray_blocks
        self.peers = n_ray * n_vox
        self.cap = 2 * slots // n_vox
        self.seg = LANES // n_ray
        self.data_rows = max(1, self.cap * self.seg // LANES)
        self.segs = self.cap // self.data_rows
        self.rows = self.data_rows + 1
        self.compact = self.cap * n_vox


def lane(shape):
    return lax.broadcasted_iota(jnp.int32, shape, len(shape) - 1)


def total(x):
    return jnp.sum(jnp.sum(x, axis=1, keepdims=True), axis=0, keepdims=True)


def pick(row, k):
    return jnp.sum(jnp.where(lane(row.shape) == k, row, 0.0), axis=1, keepdims=True)


def shift_lanes(x, amount):
    amount = amount % LANES
    return x if amount == 0 else pltpu.roll(x, amount, axis=1)


def split3(x):
    hi = x.astype(BF16)
    rest = x - hi.astype(F32)
    mid = rest.astype(BF16)
    low = (rest - mid.astype(F32)).astype(BF16)
    return jnp.concatenate([hi, mid, low], axis=1)


def select_dot(onehot, x):
    width = x.shape[1]
    out = jnp.dot(onehot, split3(x), preferred_element_type=F32)
    return out[:, :width] + out[:, width : 2 * width] + out[:, 2 * width :]


def tile_copies(tiles_hbm, tiles_v, sem, slots):
    return [
        pltpu.make_async_copy(
            tiles_hbm.at[pl.ds(c * GROUP, GROUP)], tiles_v.at[pl.ds(c * GROUP, GROUP)], sem.at[c]
        )
        for c in range(slots // GROUP)
    ]


def wait_group(tiles_hbm, tiles_v, sem, c):
    pltpu.make_async_copy(
        tiles_hbm.at[pl.ds(c * GROUP, GROUP)], tiles_v.at[pl.ds(c * GROUP, GROUP)], sem.at[c]
    ).wait()


def write_products(z, prod, msg, meta):
    segment = lane((z.n_vox, LANES)) // z.seg
    for q in range(z.data_rows):
        part = [
            prod[pl.ds((q * z.segs + g) * z.n_vox, z.n_vox), :] for g in range(z.segs)
        ]
        for r in range(z.n_ray):
            out = jnp.zeros((z.n_vox, LANES), F32)
            for g in range(z.segs):
                out = jnp.where(segment == g, shift_lanes(part[g], (g - r) * z.seg), out)
            msg[pl.ds(r * z.n_vox * z.rows + q, z.n_vox, stride=z.rows), :] = out
    for r in range(z.n_ray):
        msg[pl.ds(r * z.n_vox * z.rows + z.data_rows, z.n_vox, stride=z.rows), :] = jnp.where(
            lane((z.n_vox, LANES)) == z.cap + 1, jnp.float32(r), meta
        )


def backward(z, where_of, tiles_v, rays_wide, prod, wait):
    def step(c, carry):
        if wait is not None:
            wait(c)
        for s in range(GROUP):
            t = c * GROUP + s
            ray, row = where_of(t)
            block = rays_wide[pl.ds(ray * LANES, LANES), :]
            prod[pl.ds(row, 1), :] = jnp.sum(tiles_v[t] * block, axis=0, keepdims=True)
        return carry

    lax.fori_loop(0, z.slots // GROUP, step, 0)


def first_kernel(
    z, tile_ray, tile_vox, tile_count, travel, tiles_hbm, msg, cols, code,
    tiles_v, rays_wide, prod, named, pad, count, sem,
):
    for copy in tile_copies(tiles_hbm, tiles_v, sem, z.slots):
        copy.start()
    for o in range(z.n_vox):
        count[o] = 0
    prod[...] = jnp.zeros_like(prod)
    named[...] = jnp.full_like(named, -1.0)
    pad[...] = jnp.zeros_like(pad)
    pad[pl.ds(0, z.ray_blocks), :] = travel[...]
    by_col = pad[...].T
    cols[...] = by_col
    for r in range(z.ray_blocks):
        rays_wide[pl.ds(r * LANES, LANES), :] = jnp.broadcast_to(
            by_col[:, r : r + 1], (LANES, LANES)
        )
    live = tile_count[0]

    def where_of(t):
        vox, ray = tile_vox[t], tile_ray[t]
        owner = vox // VBD
        k = count[owner]
        count[owner] = k + 1
        row = k * z.n_vox + owner
        code[t] = row * 256 + ray
        block = jnp.where(t < live, vox - owner * VBD, -1).astype(F32)
        named[pl.ds(row, 1), :] = jnp.full((1, LANES), block, F32)
        return ray, row

    backward(
        z, where_of, tiles_v, rays_wide, prod,
        lambda c: wait_group(tiles_hbm, tiles_v, sem, c),
    )
    here = lane((z.n_vox, LANES))
    meta = jnp.where(here == z.cap, total(travel[...] * travel[...]), 0.0)
    for k in range(z.cap):
        meta = jnp.where(here == k, named[pl.ds(k * z.n_vox, z.n_vox), :], meta)
    write_products(z, prod, msg, meta)


def middle_kernel(
    z, code, back, old_cols, tiles_hbm, msg, cols, scal,
    tiles_v, rays_wide, prod, vox_rows, sums, sems, sem,
):
    for copy in tile_copies(tiles_hbm, tiles_v, sem, z.slots):
        copy.start()
    meta = back[pl.ds(z.data_rows, z.peers, stride=z.rows), :]
    alpha = jnp.sqrt(pick(jnp.sum(meta, axis=0, keepdims=True), 0))
    beta = pick(meta[0:1], 1)
    here = lane((8, LANES))
    scal[...] = jnp.where(here == 0, alpha, jnp.where(here == 1, beta, 0.0))
    segment = lane((z.n_vox, LANES)) // z.seg
    for q in range(z.data_rows):
        part = [
            back[pl.ds(r * z.n_vox * z.rows + q, z.n_vox, stride=z.rows), :]
            for r in range(z.n_ray)
        ]
        for g in range(z.segs):
            row = jnp.zeros((z.n_vox, LANES), F32)
            for r in range(z.n_ray):
                row = jnp.where(segment == r, shift_lanes(part[r], (r - g) * z.seg), row)
            vox_rows[pl.ds((q * z.segs + g) * z.n_vox, z.n_vox), :] = row / alpha
    sums[...] = jnp.zeros_like(sums)
    sems[...] = jnp.zeros_like(sems)
    prod[...] = jnp.zeros_like(prod)

    def where_of(t):
        both = code[t]
        return both & 255, both // 256

    def step(c, carry):
        wait_group(tiles_hbm, tiles_v, sem, c)
        for s in range(GROUP):
            t = c * GROUP + s
            ray, row = where_of(t)
            into = sums if s % 2 == 0 else sems
            into[pl.ds(ray * LANES, LANES), :] += tiles_v[t] * vox_rows[pl.ds(row, 1), :]
        return carry

    lax.fori_loop(0, z.slots // GROUP, step, 0)
    at = lane((LANES, LANES))
    before = old_cols[...] / beta
    now = jnp.zeros((LANES, LANES), F32)
    for r in range(z.ray_blocks):
        both = sums[pl.ds(r * LANES, LANES), :] + sems[pl.ds(r * LANES, LANES), :]
        u = jnp.sum(both, axis=1, keepdims=True) - alpha * before[:, r : r + 1]
        wide = jnp.broadcast_to(u, (LANES, LANES))
        rays_wide[pl.ds(r * LANES, LANES), :] = wide
        now = jnp.where(at == r, wide, now)
    cols[...] = now
    backward(z, where_of, tiles_v, rays_wide, prod, None)
    meta = jnp.where(lane((z.n_vox, LANES)) == z.cap, total(now * now), 0.0)
    write_products(z, prod, msg, meta)


def one_hots(z, meta, onehot, onehot_t):
    wide = jnp.concatenate(
        [shift_lanes(meta, -q * z.segs) for q in range(z.data_rows)], axis=0
    )
    n = z.data_rows * z.peers
    tall = wide.T
    block = lax.broadcasted_iota(jnp.int32, (VBD, n), 0).astype(F32)
    for g in range(z.segs):
        onehot[pl.ds(g * VBD, VBD), :] = (tall[g : g + 1, :] == block).astype(F32).astype(BF16)
    here = lane((n, LANES))
    local = (here % VBD).astype(F32)
    per = LANES // VBD
    for h in range(z.segs // per):
        named = wide[:, h * per : h * per + 1]
        for e in range(1, per):
            named = jnp.where(here // VBD == e, wide[:, h * per + e : h * per + e + 1], named)
        onehot_t[:, pl.ds(h * LANES, LANES)] = (named == local).astype(F32).astype(BF16)


def own_sum(z, msg, onehot):
    data = jnp.concatenate(
        [msg[pl.ds(q, z.peers, stride=z.rows), :] for q in range(z.data_rows)], axis=0
    )
    part = select_dot(onehot[...], data)
    segment = lane((VBD, LANES)) // z.seg
    out = jnp.zeros((VBD, LANES), F32)
    for g in range(z.segs):
        out = jnp.where(segment == g, part[g * VBD : (g + 1) * VBD], out)
    step = LANES // 2
    while step >= z.seg:
        out = out + shift_lanes(out, step)
        step //= 2
    return out


def give_back(z, y, onehot_t, beta, back):
    segment = lane((VBD, LANES)) // z.seg
    square = total(jnp.where(segment == 0, y * y, 0.0))
    spread = jnp.concatenate(
        [jnp.where(segment == g, y, 0.0) for g in range(z.segs)], axis=0
    )
    data = select_dot(onehot_t[...], spread)
    for q in range(z.data_rows):
        back[pl.ds(q, z.peers, stride=z.rows), :] = data[q * z.peers : (q + 1) * z.peers]
    here = lane((z.peers, LANES))
    back[pl.ds(z.data_rows, z.peers, stride=z.rows), :] = jnp.where(
        here == 0, square, jnp.where(here == 1, beta, 0.0)
    )


def message_beta(z, msg):
    meta = msg[pl.ds(z.data_rows, z.peers, stride=z.rows), :]
    return meta, jnp.sqrt(pick(jnp.sum(meta, axis=0, keepdims=True), z.cap))


def owner_first_kernel(z, msg, back, y_out, onehot, onehot_t):
    meta, beta = message_beta(z, msg)
    one_hots(z, meta, onehot, onehot_t)
    y = own_sum(z, msg, onehot) / beta
    y_out[...] = y
    give_back(z, y, onehot_t, beta, back)


def owner_next_kernel(z, msg, onehot, onehot_t, scal, y_in, back, y_out):
    _, beta = message_beta(z, msg)
    alpha = scal[0:1, 0:1]
    y = own_sum(z, msg, onehot) / beta - beta * (y_in[...] / alpha)
    y_out[...] = y
    give_back(z, y, onehot_t, beta, back)


def owner_last_kernel(z, msg, onehot, scal1, scal2, y1, y2, share, back):
    meta, beta3 = message_beta(z, msg)
    mine = pick(meta[0:1], z.cap + 1)
    alpha1, beta1 = scal1[0:1, 0:1], scal1[0:1, 1:2]
    alpha2, beta2 = scal2[0:1, 0:1], scal2[0:1, 1:2]
    v1, v2 = y1[...] / alpha1, y2[...] / alpha2
    w = own_sum(z, msg, onehot) / beta3 - beta3 * v2
    rho1 = jnp.sqrt(alpha1 * alpha1 + beta2 * beta2)
    c1, s1 = alpha1 / rho1, beta2 / rho1
    solution = c1 * beta1 / rho1 * v1
    direction = v2 - s1 * alpha2 / rho1 * v1
    rhobar, phibar = -c1 * alpha2, s1 * beta1
    rho2 = jnp.sqrt(rhobar * rhobar + beta3 * beta3)
    solution = solution + (rhobar / rho2) * phibar / rho2 * direction
    segment = lane((VBD, LANES)) // z.seg
    keep = segment.astype(F32) == mine
    share[pl.ds(0, VBD), :] = jnp.where(keep, w, 0.0)
    share[pl.ds(VBD, VBD), :] = jnp.where(keep, solution, 0.0)
    share[pl.ds(2 * VBD, VBD), :] = jnp.where(keep, direction, 0.0)
    here = lane((z.peers, LANES))
    square = total(jnp.where(segment == 0, w * w, 0.0))
    back[...] = jnp.where(
        here == 0, square, jnp.where(here == 1, beta3 / rho2 / rho2, 0.0)
    )


def final_kernel(z, back, *refs):
    shares, solution, direction = refs[:-2], refs[-2], refs[-1]
    whole = shares[0][...]
    for share in shares[1:]:
        whole = whole + share[...]
    alpha = jnp.sqrt(pick(jnp.sum(back[...], axis=0, keepdims=True), 0))
    factor = pick(back[0:1, :], 1) * alpha
    solution[...] = whole[VBD : 2 * VBD]
    direction[...] = whole[:VBD] / alpha - factor * whole[2 * VBD :]


SMEM = pl.BlockSpec(memory_space=pltpu.SMEM)
VMEM = pl.BlockSpec(memory_space=pltpu.VMEM)
ANY = pl.BlockSpec(memory_space=pl.ANY)
PARAMS = pltpu.CompilerParams(vmem_limit_bytes=24 * 1024 * 1024)


def f32(*shape):
    return jax.ShapeDtypeStruct(shape, F32)


def on_device(tiles, tile_ray, tile_vox, tile_count, travel):
    n_ray, n_vox = lax.axis_size("ray"), lax.axis_size("vox")
    z = Sizes(n_ray, n_vox, tiles.shape[0], travel.shape[0])
    message = f32(z.peers * z.rows, LANES)
    square = f32(LANES, LANES)
    owned = f32(VBD, LANES)

    def call(kernel, name, in_specs, out_shape, out_specs, *args, scratch=()):
        return pl.pallas_call(
            functools.partial(kernel, z), name=name, in_specs=in_specs, out_shape=out_shape,
            out_specs=out_specs, scratch_shapes=scratch, compiler_params=PARAMS,
        )(*args)

    def exchange(x):
        n = x.shape[0]
        out = lax.all_to_all(x.reshape(n, 1, LANES), ("ray", "vox"), 0, 0, tiled=True)
        return out.reshape(n, LANES)

    tiles_v = pltpu.VMEM(tiles.shape, F32)
    per_ray = pltpu.VMEM((z.ray_blocks * LANES, LANES), F32)
    compact = pltpu.VMEM((z.compact, LANES), F32)
    sem = pltpu.SemaphoreType.DMA((z.slots // GROUP,))

    def middle(code, back, cols, name):
        return call(
            middle_kernel, name, [SMEM, VMEM, VMEM, ANY], (message, square, f32(8, LANES)),
            (VMEM, VMEM, VMEM), code, back, cols, tiles,
            scratch=(tiles_v, per_ray, compact, compact, per_ray, per_ray, sem),
        )

    msg, cols, code = call(
        first_kernel, "first", [SMEM, SMEM, SMEM, VMEM, ANY],
        (message, square, jax.ShapeDtypeStruct((z.slots,), jnp.int32)), (VMEM, VMEM, SMEM),
        tile_ray, tile_vox, tile_count, travel, tiles,
        scratch=(
            tiles_v, per_ray, compact, compact, pltpu.VMEM((LANES, LANES), F32),
            pltpu.SMEM((z.n_vox,), jnp.int32), sem,
        ),
    )
    n, m = z.data_rows * z.peers, z.segs * VBD
    back, y1, onehot, onehot_t = call(
        owner_first_kernel, "owner1", [VMEM],
        (message, owned, jax.ShapeDtypeStruct((m, n), BF16), jax.ShapeDtypeStruct((n, m), BF16)),
        (VMEM,) * 4, exchange(msg),
    )
    msg, cols, scal1 = middle(code, exchange(back), cols, "middle1")
    back, y2 = call(
        owner_next_kernel, "owner2", [VMEM] * 5, (message, owned), (VMEM,) * 2,
        exchange(msg), onehot, onehot_t, scal1, y1,
    )
    msg, cols, scal2 = middle(code, exchange(back), cols, "middle2")
    share, back = call(
        owner_last_kernel, "owner3", [VMEM] * 6, (f32(3 * VBD, LANES), f32(z.peers, LANES)),
        (VMEM,) * 2, exchange(msg), onehot, scal1, scal2, y1, y2,
    )
    shares = [share]
    hop = 1
    while hop < n_ray:
        pairs = [(r, r ^ hop) for r in range(n_ray)]
        shares = shares + [lax.ppermute(s, "ray", pairs) for s in shares]
        hop *= 2
    return call(
        final_kernel, "final", [VMEM] * (1 + n_ray), (owned, owned), (VMEM,) * 2,
        exchange(back), *shares,
    )


def solution(mesh):
    return jax.shard_map(
        on_device,
        mesh=mesh,
        in_specs=(
            P(("ray", "vox"), None, None),
            P(("ray", "vox")),
            P(("ray", "vox")),
            P(("ray", "vox")),
            P(("ray", "vox"), None),
        ),
        out_specs=(P("vox", None), P("vox", None)),
        check_vma=False,
    )
```

```python
import functools

import jax
import jax.numpy as jnp
from jax import lax
from jax.experimental import pallas as pl
from jax.experimental.pallas import tpu as pltpu
from jax.sharding import PartitionSpec as P

VBD = 64
LANES = 128
GROUP = 8
AHEAD = 8
F32 = jnp.float32
BF16 = jnp.bfloat16


class Sizes:
    def __init__(self, n_ray, n_vox, slots, ray_blocks):
        self.n_ray, self.n_vox, self.slots, self.ray_blocks = n_ray, n_vox, slots, ray_blocks
        self.peers = n_ray * n_vox
        self.cap = 2 * slots // n_vox
        self.seg = LANES // n_ray
        self.data_rows = max(1, self.cap * self.seg // LANES)
        self.segs = self.cap // self.data_rows
        self.rows = self.data_rows + 1
        self.compact = self.cap * n_vox


def lane(shape):
    return lax.broadcasted_iota(jnp.int32, shape, len(shape) - 1)


def total(x):
    return jnp.sum(jnp.sum(x, axis=1, keepdims=True), axis=0, keepdims=True)


def pick(row, k):
    return jnp.sum(jnp.where(lane(row.shape) == k, row, 0.0), axis=1, keepdims=True)


def shift_lanes(x, amount):
    amount = amount % LANES
    return x if amount == 0 else pltpu.roll(x, amount, axis=1)


def split3(x):
    hi = x.astype(BF16)
    rest = x - hi.astype(F32)
    mid = rest.astype(BF16)
    low = (rest - mid.astype(F32)).astype(BF16)
    return jnp.concatenate([hi, mid, low], axis=1)


def select_dot(onehot, x):
    width = x.shape[1]
    out = jnp.dot(onehot, split3(x), preferred_element_type=F32)
    return out[:, :width] + out[:, width : 2 * width] + out[:, 2 * width :]


def tile_copy(tiles_hbm, tiles_v, sem, c):
    part = pl.ds(c * GROUP, GROUP)
    return pltpu.make_async_copy(tiles_hbm.at[part], tiles_v.at[part], sem.at[c])


def write_products(z, prod, msg, meta):
    segment = lane((z.n_vox, LANES)) // z.seg
    for q in range(z.data_rows):
        part = [
            prod[pl.ds((q * z.segs + g) * z.n_vox, z.n_vox), :] for g in range(z.segs)
        ]
        for r in range(z.n_ray):
            out = jnp.zeros((z.n_vox, LANES), F32)
            for g in range(z.segs):
                out = jnp.where(segment == g, shift_lanes(part[g], (g - r) * z.seg), out)
            msg[pl.ds(r * z.n_vox * z.rows + q, z.n_vox, stride=z.rows), :] = out
    for r in range(z.n_ray):
        msg[pl.ds(r * z.n_vox * z.rows + z.data_rows, z.n_vox, stride=z.rows), :] = jnp.where(
            lane((z.n_vox, LANES)) == z.cap + 1, jnp.float32(r), meta
        )


def backward(z, where_of, tiles_v, wide, prod, ready=None):
    def step(c, carry):
        if ready is not None:
            ready(c)
        for s in range(GROUP):
            t = c * GROUP + s
            ray, row = where_of(t)
            prod[pl.ds(row, 1), :] = jnp.sum(tiles_v[t] * wide[ray], axis=0, keepdims=True)
        return carry

    lax.fori_loop(0, z.slots // GROUP, step, 0)


def first_kernel(
    z, ray_hbm, vox_hbm, tile_count, travel_hbm, tiles_hbm, msg, wide, code_out, tiles_v,
    prod, named, pad, tile_ray, tile_vox, travel, code, count, sem, small_sem, code_sem,
):
    small = [
        pltpu.make_async_copy(src, dst, small_sem.at[i])
        for i, (src, dst) in enumerate(
            [(ray_hbm, tile_ray), (vox_hbm, tile_vox), (travel_hbm, travel)]
        )
    ]
    groups = z.slots // GROUP
    for copy in small:
        copy.start()
    for c in range(min(AHEAD, groups)):
        tile_copy(tiles_hbm, tiles_v, sem, c).start()
    for o in range(z.n_vox):
        count[o] = 0
    prod[...] = jnp.zeros_like(prod)
    named[...] = jnp.full_like(named, -1.0)
    pad[...] = jnp.zeros_like(pad)
    for copy in small:
        copy.wait()
    pad[pl.ds(0, z.ray_blocks), :] = travel[...]
    by_col = pad[...].T
    for r in range(z.ray_blocks):
        wide[r] = jnp.broadcast_to(by_col[:, r : r + 1], (LANES, LANES))
    live = tile_count[0]

    def ready(c):
        tile_copy(tiles_hbm, tiles_v, sem, c).wait()

        @pl.when(c + AHEAD < groups)
        def _():
            tile_copy(tiles_hbm, tiles_v, sem, c + AHEAD).start()

    def where_of(t):
        vox, ray = tile_vox[t], tile_ray[t]
        owner = lax.shift_right_logical(vox, VBD.bit_length() - 1)
        k = count[owner]
        count[owner] = k + 1
        row = k * z.n_vox + owner
        code[t] = row * 256 + ray
        block = jnp.where(t < live, vox & (VBD - 1), -1).astype(F32)
        named[pl.ds(row, 1), :] = jnp.full((1, LANES), block, F32)
        return ray, row

    backward(z, where_of, tiles_v, wide, prod, ready)
    keep = pltpu.make_async_copy(code, code_out, code_sem)
    keep.start()
    here = lane((z.n_vox, LANES))
    meta = jnp.where(here == z.cap, total(travel[...] * travel[...]), 0.0)
    for k in range(z.cap):
        meta = jnp.where(here == k, named[pl.ds(k * z.n_vox, z.n_vox), :], meta)
    write_products(z, prod, msg, meta)
    keep.wait()


def middle_kernel(
    z, code_v, back, old, tiles_v, msg, scal, *refs
):
    wide, prod, vox_rows, sums, sems, code, code_sem = refs
    fetch = pltpu.make_async_copy(code_v, code, code_sem)
    fetch.start()
    meta = back[pl.ds(z.data_rows, z.peers, stride=z.rows), :]
    alpha = jnp.sqrt(pick(jnp.sum(meta, axis=0, keepdims=True), 0))
    beta = pick(meta[0:1], 1)
    here = lane((8, LANES))
    scal[...] = jnp.where(here == 0, alpha, jnp.where(here == 1, beta, 0.0))
    segment = lane((z.n_vox, LANES)) // z.seg
    for q in range(z.data_rows):
        part = [
            back[pl.ds(r * z.n_vox * z.rows + q, z.n_vox, stride=z.rows), :]
            for r in range(z.n_ray)
        ]
        for g in range(z.segs):
            row = jnp.zeros((z.n_vox, LANES), F32)
            for r in range(z.n_ray):
                row = jnp.where(segment == r, shift_lanes(part[r], (r - g) * z.seg), row)
            vox_rows[pl.ds((q * z.segs + g) * z.n_vox, z.n_vox), :] = row / alpha
    lane_share = -alpha / beta * (1.0 / LANES)
    for r in range(z.ray_blocks):
        sums[r] = old[r] * lane_share
        sems[r] = jnp.zeros((LANES, LANES), F32)
    prod[...] = jnp.zeros_like(prod)
    fetch.wait()

    def where_of(t):
        both = code[t]
        return both & 255, lax.shift_right_logical(both, 8)

    def step(c, carry):
        for s in range(GROUP):
            t = c * GROUP + s
            ray, row = where_of(t)
            into = sums if s % 2 == 0 else sems
            into[ray] += tiles_v[t] * vox_rows[pl.ds(row, 1), :]
        return carry

    lax.fori_loop(0, z.slots // GROUP, step, 0)
    square = jnp.zeros((LANES, LANES), F32)
    for r in range(z.ray_blocks):
        u = jnp.broadcast_to(
            jnp.sum(sums[r] + sems[r], axis=1, keepdims=True), (LANES, LANES)
        )
        wide[r] = u
        square += u * u
    backward(z, where_of, tiles_v, wide, prod)
    meta = jnp.where(
        lane((z.n_vox, LANES)) == z.cap, total(square) * (1.0 / LANES), 0.0
    )
    write_products(z, prod, msg, meta)


def one_hots(z, meta, onehot, onehot_t):
    wide = jnp.concatenate(
        [shift_lanes(meta, -q * z.segs) for q in range(z.data_rows)], axis=0
    )
    n = z.data_rows * z.peers
    tall = wide.T
    block = lax.broadcasted_iota(jnp.int32, (VBD, n), 0).astype(F32)
    for g in range(z.segs):
        onehot[pl.ds(g * VBD, VBD), :] = (tall[g : g + 1, :] == block).astype(F32).astype(BF16)
    here = lane((n, LANES))
    local = (here % VBD).astype(F32)
    per = LANES // VBD
    for h in range(z.segs // per):
        named = wide[:, h * per : h * per + 1]
        for e in range(1, per):
            named = jnp.where(here // VBD == e, wide[:, h * per + e : h * per + e + 1], named)
        onehot_t[:, pl.ds(h * LANES, LANES)] = (named == local).astype(F32).astype(BF16)


def own_sum(z, msg, onehot):
    data = jnp.concatenate(
        [msg[pl.ds(q, z.peers, stride=z.rows), :] for q in range(z.data_rows)], axis=0
    )
    part = select_dot(onehot[...], data)
    segment = lane((VBD, LANES)) // z.seg
    out = jnp.zeros((VBD, LANES), F32)
    for g in range(z.segs):
        out = jnp.where(segment == g, part[g * VBD : (g + 1) * VBD], out)
    step = LANES // 2
    while step >= z.seg:
        out = out + shift_lanes(out, step)
        step //= 2
    return out


def give_back(z, y, onehot_t, beta, back):
    segment = lane((VBD, LANES)) // z.seg
    square = total(jnp.where(segment == 0, y * y, 0.0))
    spread = jnp.concatenate(
        [jnp.where(segment == g, y, 0.0) for g in range(z.segs)], axis=0
    )
    data = select_dot(onehot_t[...], spread)
    for q in range(z.data_rows):
        back[pl.ds(q, z.peers, stride=z.rows), :] = data[q * z.peers : (q + 1) * z.peers]
    here = lane((z.peers, LANES))
    back[pl.ds(z.data_rows, z.peers, stride=z.rows), :] = jnp.where(
        here == 0, square, jnp.where(here == 1, beta, 0.0)
    )


def message_beta(z, msg):
    meta = msg[pl.ds(z.data_rows, z.peers, stride=z.rows), :]
    return meta, jnp.sqrt(pick(jnp.sum(meta, axis=0, keepdims=True), z.cap))


def owner_first_kernel(z, msg, back, y_out, onehot, onehot_t):
    meta, beta = message_beta(z, msg)
    one_hots(z, meta, onehot, onehot_t)
    y = own_sum(z, msg, onehot) / beta
    y_out[...] = y
    give_back(z, y, onehot_t, beta, back)


def owner_next_kernel(z, msg, onehot, onehot_t, scal, y_in, back, y_out):
    _, beta = message_beta(z, msg)
    alpha = scal[0:1, 0:1]
    y = own_sum(z, msg, onehot) / beta - beta * (y_in[...] / alpha)
    y_out[...] = y
    give_back(z, y, onehot_t, beta, back)


def owner_last_kernel(z, msg, onehot, scal1, scal2, y1, y2, share, back):
    meta, beta3 = message_beta(z, msg)
    mine = pick(meta[0:1], z.cap + 1)
    alpha1, beta1 = scal1[0:1, 0:1], scal1[0:1, 1:2]
    alpha2, beta2 = scal2[0:1, 0:1], scal2[0:1, 1:2]
    v1, v2 = y1[...] / alpha1, y2[...] / alpha2
    w = own_sum(z, msg, onehot) / beta3 - beta3 * v2
    rho1 = jnp.sqrt(alpha1 * alpha1 + beta2 * beta2)
    c1, s1 = alpha1 / rho1, beta2 / rho1
    solution = c1 * beta1 / rho1 * v1
    direction = v2 - s1 * alpha2 / rho1 * v1
    rhobar, phibar = -c1 * alpha2, s1 * beta1
    rho2 = jnp.sqrt(rhobar * rhobar + beta3 * beta3)
    solution = solution + (rhobar / rho2) * phibar / rho2 * direction
    segment = lane((VBD, LANES)) // z.seg
    keep = segment.astype(F32) == mine
    share[pl.ds(0, VBD), :] = jnp.where(keep, w, 0.0)
    share[pl.ds(VBD, VBD), :] = jnp.where(keep, solution, 0.0)
    share[pl.ds(2 * VBD, VBD), :] = jnp.where(keep, direction, 0.0)
    here = lane((z.peers, LANES))
    square = total(jnp.where(segment == 0, w * w, 0.0))
    back[...] = jnp.where(
        here == 0, square, jnp.where(here == 1, beta3 / rho2 / rho2, 0.0)
    )


def final_kernel(z, back, *refs):
    shares, solution, direction = refs[:-2], refs[-2], refs[-1]
    whole = shares[0][...]
    for share in shares[1:]:
        whole = whole + share[...]
    alpha = jnp.sqrt(pick(jnp.sum(back[...], axis=0, keepdims=True), 0))
    factor = pick(back[0:1, :], 1) * alpha
    solution[...] = whole[VBD : 2 * VBD]
    direction[...] = whole[:VBD] / alpha - factor * whole[2 * VBD :]


SMEM = pl.BlockSpec(memory_space=pltpu.SMEM)
VMEM = pl.BlockSpec(memory_space=pltpu.VMEM)
HBM = pl.BlockSpec(memory_space=pltpu.HBM)
PARAMS = pltpu.CompilerParams(vmem_limit_bytes=24 * 1024 * 1024)


def in_hbm(x):
    return pltpu.with_memory_space_constraint(x, pltpu.HBM)


def f32(*shape):
    return jax.ShapeDtypeStruct(shape, F32)


def on_device(tiles, tile_ray, tile_vox, tile_count, travel):
    n_ray, n_vox = lax.axis_size("ray"), lax.axis_size("vox")
    z = Sizes(n_ray, n_vox, tiles.shape[0], travel.shape[0])
    message = f32(z.peers * z.rows, LANES)
    wide_rays = f32(z.ray_blocks, LANES, LANES)
    owned = f32(VBD, LANES)

    def call(kernel, name, in_specs, out_shape, out_specs, *args, scratch=()):
        return pl.pallas_call(
            functools.partial(kernel, z), name=name, in_specs=in_specs, out_shape=out_shape,
            out_specs=out_specs, scratch_shapes=scratch, compiler_params=PARAMS,
        )(*args)

    def exchange(x):
        n = x.shape[0]
        out = lax.all_to_all(x.reshape(n, 1, LANES), ("ray", "vox"), 0, 0, tiled=True)
        return out.reshape(n, LANES)

    per_ray = pltpu.VMEM((z.ray_blocks, LANES, LANES), F32)
    compact = pltpu.VMEM((z.compact, LANES), F32)
    indices = pltpu.SMEM((z.slots,), jnp.int32)
    one_sem = pltpu.SemaphoreType.DMA(())

    def middle(back, wide, last):
        scratch = (compact, compact, per_ray, per_ray, indices, one_sem)
        out = (message, f32(8, LANES))
        return call(
            middle_kernel, "middle2" if last else "middle1", (VMEM,) * 4,
            out if last else out + (wide_rays,), (VMEM,) * (2 if last else 3),
            code, back, wide, tiles_v, scratch=(per_ray,) + scratch if last else scratch,
        )

    msg, wide, code, tiles_v = call(
        first_kernel, "first", [HBM, HBM, SMEM, HBM, HBM],
        (message, wide_rays, jax.ShapeDtypeStruct((z.slots,), jnp.int32), f32(*tiles.shape)),
        (VMEM,) * 4,
        in_hbm(tile_ray), in_hbm(tile_vox), tile_count, in_hbm(travel), in_hbm(tiles),
        scratch=(
            compact, compact, pltpu.VMEM((LANES, LANES), F32), indices, indices,
            pltpu.VMEM(travel.shape, F32), indices, pltpu.SMEM((z.n_vox,), jnp.int32),
            pltpu.SemaphoreType.DMA((z.slots // GROUP,)), pltpu.SemaphoreType.DMA((3,)), one_sem,
        ),
    )
    n, m = z.data_rows * z.peers, z.segs * VBD
    back, y1, onehot, onehot_t = call(
        owner_first_kernel, "owner1", [VMEM],
        (message, owned, jax.ShapeDtypeStruct((m, n), BF16), jax.ShapeDtypeStruct((n, m), BF16)),
        (VMEM,) * 4, exchange(msg),
    )
    msg, scal1, wide = middle(exchange(back), wide, False)
    back, y2 = call(
        owner_next_kernel, "owner2", [VMEM] * 5, (message, owned), (VMEM,) * 2,
        exchange(msg), onehot, onehot_t, scal1, y1,
    )
    msg, scal2 = middle(exchange(back), wide, True)
    share, back = call(
        owner_last_kernel, "owner3", [VMEM] * 6, (f32(3 * VBD, LANES), f32(z.peers, LANES)),
        (VMEM,) * 2, exchange(msg), onehot, scal1, scal2, y1, y2,
    )
    shares = [share]
    hop = 1
    while hop < n_ray:
        pairs = [(r, r ^ hop) for r in range(n_ray)]
        shares = shares + [lax.ppermute(s, "ray", pairs) for s in shares]
        hop *= 2
    return call(
        final_kernel, "final", [VMEM] * (1 + n_ray), (owned, owned), (VMEM,) * 2,
        exchange(back), *shares,
    )


def solution(mesh):
    return jax.shard_map(
        on_device,
        mesh=mesh,
        in_specs=(
            P(("ray", "vox"), None, None),
            P(("ray", "vox")),
            P(("ray", "vox")),
            P(("ray", "vox")),
            P(("ray", "vox"), None),
        ),
        out_specs=(P("vox", None), P("vox", None)),
        check_vma=False,
    )
```

```python
import functools

import jax
import jax.numpy as jnp
from jax import lax
from jax.experimental import pallas as pl
from jax.experimental.pallas import tpu as pltpu
from jax.sharding import PartitionSpec as P

VBD = 64
LANES = 128
GROUP = 8
F32 = jnp.float32
BF16 = jnp.bfloat16


class Sizes:
    def __init__(self, n_ray, n_vox, slots, ray_blocks):
        self.n_ray, self.n_vox, self.slots, self.ray_blocks = n_ray, n_vox, slots, ray_blocks
        self.peers = n_ray * n_vox
        self.cap = 2 * slots // n_vox
        self.seg = LANES // n_ray
        self.data_rows = max(1, self.cap * self.seg // LANES)
        self.segs = self.cap // self.data_rows
        self.rows = self.data_rows + 1
        self.compact = self.cap * n_vox


def lane(shape):
    return lax.broadcasted_iota(jnp.int32, shape, len(shape) - 1)


def total(x):
    return jnp.sum(jnp.sum(x, axis=1, keepdims=True), axis=0, keepdims=True)


def pick(row, k):
    return jnp.sum(jnp.where(lane(row.shape) == k, row, 0.0), axis=1, keepdims=True)


def shift_lanes(x, amount):
    amount = amount % LANES
    return x if amount == 0 else pltpu.roll(x, amount, axis=1)


def split3(x):
    hi = x.astype(BF16)
    rest = x - hi.astype(F32)
    mid = rest.astype(BF16)
    low = (rest - mid.astype(F32)).astype(BF16)
    return jnp.concatenate([hi, mid, low], axis=1)


def select_dot(onehot, x):
    width = x.shape[1]
    out = jnp.dot(onehot, split3(x), preferred_element_type=F32)
    return out[:, :width] + out[:, width : 2 * width] + out[:, 2 * width :]


def tile_copy(tiles_hbm, tiles_v, sem, c):
    part = pl.ds(c * GROUP, GROUP)
    return pltpu.make_async_copy(tiles_hbm.at[part], tiles_v.at[part], sem.at[c])


def write_products(z, prod, msg, meta):
    segment = lane((z.n_vox, LANES)) // z.seg
    for q in range(z.data_rows):
        part = [
            prod[pl.ds((q * z.segs + g) * z.n_vox, z.n_vox), :] for g in range(z.segs)
        ]
        for r in range(z.n_ray):
            out = jnp.zeros((z.n_vox, LANES), F32)
            for g in range(z.segs):
                out = jnp.where(segment == g, shift_lanes(part[g], (g - r) * z.seg), out)
            msg[pl.ds(r * z.n_vox * z.rows + q, z.n_vox, stride=z.rows), :] = out
    for r in range(z.n_ray):
        msg[pl.ds(r * z.n_vox * z.rows + z.data_rows, z.n_vox, stride=z.rows), :] = jnp.where(
            lane((z.n_vox, LANES)) == z.cap + 1, jnp.float32(r), meta
        )


def backward(groups, where_of, tiles_v, wide, prod, ready=None):
    def step(c, carry):
        if ready is not None:
            ready(c)
        for s in range(GROUP):
            t = c * GROUP + s
            ray, row = where_of(t)
            prod[pl.ds(row, 1), :] = jnp.sum(tiles_v[t] * wide[ray], axis=0, keepdims=True)
        return carry

    lax.fori_loop(0, groups, step, 0)


def first_kernel(
    z, ray_hbm, vox_hbm, tile_count, travel_hbm, tiles_hbm, msg, wide, code_out, tiles_v,
    prod, named, pad, tile_ray, tile_vox, travel, code, count, sem, small_sem, code_sem,
):
    small = [
        pltpu.make_async_copy(src, dst, small_sem.at[i])
        for i, (src, dst) in enumerate(
            [(travel_hbm, travel), (ray_hbm, tile_ray), (vox_hbm, tile_vox)]
        )
    ]
    live = tile_count[0]
    groups = lax.shift_right_logical(live + (GROUP - 1), GROUP.bit_length() - 1)
    for copy in small:
        copy.start()
    for c in range(z.slots // GROUP):

        @pl.when(c < groups)
        def _():
            tile_copy(tiles_hbm, tiles_v, sem, c).start()

    for o in range(z.n_vox):
        count[o] = 0
    prod[...] = jnp.zeros_like(prod)
    named[...] = jnp.full_like(named, -1.0)
    pad[...] = jnp.zeros_like(pad)
    small[0].wait()
    pad[pl.ds(0, z.ray_blocks), :] = travel[...]
    by_col = pad[...].T
    for r in range(z.ray_blocks):
        wide[r] = jnp.broadcast_to(by_col[:, r : r + 1], (LANES, LANES))
    for copy in small[1:]:
        copy.wait()

    def ready(c):
        tile_copy(tiles_hbm, tiles_v, sem, c).wait()

    def where_of(t):
        vox, ray = tile_vox[t], tile_ray[t]
        owner = lax.shift_right_logical(vox, VBD.bit_length() - 1)
        k = count[owner]
        count[owner] = k + 1
        row = k * z.n_vox + owner
        code[t] = row * 256 + ray
        block = jnp.where(t < live, vox & (VBD - 1), -1).astype(F32)
        named[pl.ds(row, 1), :] = jnp.full((1, LANES), block, F32)
        return ray, row

    code[z.slots] = groups
    backward(groups, where_of, tiles_v, wide, prod, ready)
    keep = pltpu.make_async_copy(code, code_out, code_sem)
    keep.start()
    here = lane((z.n_vox, LANES))
    meta = jnp.where(here == z.cap, total(travel[...] * travel[...]), 0.0)
    for k in range(z.cap):
        meta = jnp.where(here == k, named[pl.ds(k * z.n_vox, z.n_vox), :], meta)
    write_products(z, prod, msg, meta)
    keep.wait()


def middle_kernel(
    z, code_v, back, old, tiles_v, msg, scal, *refs
):
    wide, prod, vox_rows, sums, sems, code, code_sem = refs
    fetch = pltpu.make_async_copy(code_v, code, code_sem)
    fetch.start()
    meta = back[pl.ds(z.data_rows, z.peers, stride=z.rows), :]
    alpha = jnp.sqrt(pick(jnp.sum(meta, axis=0, keepdims=True), 0))
    beta = pick(meta[0:1], 1)
    here = lane((8, LANES))
    scal[...] = jnp.where(here == 0, alpha, jnp.where(here == 1, beta, 0.0))
    segment = lane((z.n_vox, LANES)) // z.seg
    for q in range(z.data_rows):
        part = [
            back[pl.ds(r * z.n_vox * z.rows + q, z.n_vox, stride=z.rows), :]
            for r in range(z.n_ray)
        ]
        for g in range(z.segs):
            row = jnp.zeros((z.n_vox, LANES), F32)
            for r in range(z.n_ray):
                row = jnp.where(segment == r, shift_lanes(part[r], (r - g) * z.seg), row)
            vox_rows[pl.ds((q * z.segs + g) * z.n_vox, z.n_vox), :] = row / alpha
    lane_share = -alpha / beta * (1.0 / LANES)
    for r in range(z.ray_blocks):
        sums[r] = old[r] * lane_share
        sems[r] = jnp.zeros((LANES, LANES), F32)
    prod[...] = jnp.zeros_like(prod)
    fetch.wait()
    groups = code[z.slots]

    def where_of(t):
        both = code[t]
        return both & 255, lax.shift_right_logical(both, 8)

    def step(c, carry):
        for s in range(GROUP):
            t = c * GROUP + s
            ray, row = where_of(t)
            into = sums if s % 2 == 0 else sems
            into[ray] += tiles_v[t] * vox_rows[pl.ds(row, 1), :]
        return carry

    lax.fori_loop(0, groups, step, 0)
    square = jnp.zeros((LANES, LANES), F32)
    for r in range(z.ray_blocks):
        u = jnp.broadcast_to(
            jnp.sum(sums[r] + sems[r], axis=1, keepdims=True), (LANES, LANES)
        )
        wide[r] = u
        square += u * u
    backward(groups, where_of, tiles_v, wide, prod)
    meta = jnp.where(
        lane((z.n_vox, LANES)) == z.cap, total(square) * (1.0 / LANES), 0.0
    )
    write_products(z, prod, msg, meta)


def one_hots(z, meta, onehot, onehot_t):
    wide = jnp.concatenate(
        [shift_lanes(meta, -q * z.segs) for q in range(z.data_rows)], axis=0
    )
    n = z.data_rows * z.peers
    tall = wide.T
    block = lax.broadcasted_iota(jnp.int32, (VBD, n), 0).astype(F32)
    for g in range(z.segs):
        onehot[pl.ds(g * VBD, VBD), :] = (tall[g : g + 1, :] == block).astype(F32).astype(BF16)
    here = lane((n, LANES))
    local = (here % VBD).astype(F32)
    per = LANES // VBD
    for h in range(z.segs // per):
        named = wide[:, h * per : h * per + 1]
        for e in range(1, per):
            named = jnp.where(here // VBD == e, wide[:, h * per + e : h * per + e + 1], named)
        onehot_t[:, pl.ds(h * LANES, LANES)] = (named == local).astype(F32).astype(BF16)


def own_sum(z, msg, onehot):
    data = jnp.concatenate(
        [msg[pl.ds(q, z.peers, stride=z.rows), :] for q in range(z.data_rows)], axis=0
    )
    part = select_dot(onehot[...], data)
    segment = lane((VBD, LANES)) // z.seg
    out = jnp.zeros((VBD, LANES), F32)
    for g in range(z.segs):
        out = jnp.where(segment == g, part[g * VBD : (g + 1) * VBD], out)
    step = LANES // 2
    while step >= z.seg:
        out = out + shift_lanes(out, step)
        step //= 2
    return out


def give_back(z, y, onehot_t, beta, back):
    segment = lane((VBD, LANES)) // z.seg
    square = total(jnp.where(segment == 0, y * y, 0.0))
    spread = jnp.concatenate(
        [jnp.where(segment == g, y, 0.0) for g in range(z.segs)], axis=0
    )
    data = select_dot(onehot_t[...], spread)
    for q in range(z.data_rows):
        back[pl.ds(q, z.peers, stride=z.rows), :] = data[q * z.peers : (q + 1) * z.peers]
    here = lane((z.peers, LANES))
    back[pl.ds(z.data_rows, z.peers, stride=z.rows), :] = jnp.where(
        here == 0, square, jnp.where(here == 1, beta, 0.0)
    )


def message_beta(z, msg):
    meta = msg[pl.ds(z.data_rows, z.peers, stride=z.rows), :]
    return meta, jnp.sqrt(pick(jnp.sum(meta, axis=0, keepdims=True), z.cap))


def owner_first_kernel(z, msg, back, y_out, onehot, onehot_t):
    meta, beta = message_beta(z, msg)
    one_hots(z, meta, onehot, onehot_t)
    y = own_sum(z, msg, onehot) / beta
    y_out[...] = y
    give_back(z, y, onehot_t, beta, back)


def owner_next_kernel(z, msg, onehot, onehot_t, scal, y_in, back, y_out):
    _, beta = message_beta(z, msg)
    alpha = scal[0:1, 0:1]
    y = own_sum(z, msg, onehot) / beta - beta * (y_in[...] / alpha)
    y_out[...] = y
    give_back(z, y, onehot_t, beta, back)


def owner_last_kernel(z, msg, onehot, scal1, scal2, y1, y2, share, back):
    meta, beta3 = message_beta(z, msg)
    mine = pick(meta[0:1], z.cap + 1)
    alpha1, beta1 = scal1[0:1, 0:1], scal1[0:1, 1:2]
    alpha2, beta2 = scal2[0:1, 0:1], scal2[0:1, 1:2]
    v1, v2 = y1[...] / alpha1, y2[...] / alpha2
    w = own_sum(z, msg, onehot) / beta3 - beta3 * v2
    rho1 = jnp.sqrt(alpha1 * alpha1 + beta2 * beta2)
    c1, s1 = alpha1 / rho1, beta2 / rho1
    solution = c1 * beta1 / rho1 * v1
    direction = v2 - s1 * alpha2 / rho1 * v1
    rhobar, phibar = -c1 * alpha2, s1 * beta1
    rho2 = jnp.sqrt(rhobar * rhobar + beta3 * beta3)
    solution = solution + (rhobar / rho2) * phibar / rho2 * direction
    segment = lane((VBD, LANES)) // z.seg
    keep = segment.astype(F32) == mine
    share[pl.ds(0, VBD), :] = jnp.where(keep, w, 0.0)
    share[pl.ds(VBD, VBD), :] = jnp.where(keep, solution, 0.0)
    share[pl.ds(2 * VBD, VBD), :] = jnp.where(keep, direction, 0.0)
    here = lane((z.peers, LANES))
    square = total(jnp.where(segment == 0, w * w, 0.0))
    back[...] = jnp.where(
        here == 0, square, jnp.where(here == 1, beta3 / rho2 / rho2, 0.0)
    )


def final_kernel(z, back, *refs):
    shares, solution, direction = refs[:-2], refs[-2], refs[-1]
    whole = shares[0][...]
    for share in shares[1:]:
        whole = whole + share[...]
    alpha = jnp.sqrt(pick(jnp.sum(back[...], axis=0, keepdims=True), 0))
    factor = pick(back[0:1, :], 1) * alpha
    solution[...] = whole[VBD : 2 * VBD]
    direction[...] = whole[:VBD] / alpha - factor * whole[2 * VBD :]


SMEM = pl.BlockSpec(memory_space=pltpu.SMEM)
VMEM = pl.BlockSpec(memory_space=pltpu.VMEM)
HBM = pl.BlockSpec(memory_space=pltpu.HBM)
PARAMS = pltpu.CompilerParams(vmem_limit_bytes=24 * 1024 * 1024)


def in_hbm(x):
    return pltpu.with_memory_space_constraint(x, pltpu.HBM)


def f32(*shape):
    return jax.ShapeDtypeStruct(shape, F32)


def on_device(tiles, tile_ray, tile_vox, tile_count, travel):
    n_ray, n_vox = lax.axis_size("ray"), lax.axis_size("vox")
    z = Sizes(n_ray, n_vox, tiles.shape[0], travel.shape[0])
    message = f32(z.peers * z.rows, LANES)
    wide_rays = f32(z.ray_blocks, LANES, LANES)
    owned = f32(VBD, LANES)

    def call(kernel, name, in_specs, out_shape, out_specs, *args, scratch=()):
        return pl.pallas_call(
            functools.partial(kernel, z), name=name, in_specs=in_specs, out_shape=out_shape,
            out_specs=out_specs, scratch_shapes=scratch, compiler_params=PARAMS,
        )(*args)

    def exchange(x):
        n = x.shape[0]
        out = lax.all_to_all(x.reshape(n, 1, LANES), ("ray", "vox"), 0, 0, tiled=True)
        return out.reshape(n, LANES)

    per_ray = pltpu.VMEM((z.ray_blocks, LANES, LANES), F32)
    compact = pltpu.VMEM((z.compact, LANES), F32)
    indices = pltpu.SMEM((z.slots,), jnp.int32)
    codes = pltpu.SMEM((z.slots + 1,), jnp.int32)
    one_sem = pltpu.SemaphoreType.DMA(())

    def middle(back, wide, last):
        scratch = (compact, compact, per_ray, per_ray, codes, one_sem)
        out = (message, f32(8, LANES))
        return call(
            middle_kernel, "middle2" if last else "middle1", (VMEM,) * 4,
            out if last else out + (wide_rays,), (VMEM,) * (2 if last else 3),
            code, back, wide, tiles_v, scratch=(per_ray,) + scratch if last else scratch,
        )

    msg, wide, code, tiles_v = call(
        first_kernel, "first", [HBM, HBM, SMEM, HBM, HBM],
        (message, wide_rays, jax.ShapeDtypeStruct((z.slots + 1,), jnp.int32), f32(*tiles.shape)),
        (VMEM,) * 4,
        in_hbm(tile_ray), in_hbm(tile_vox), tile_count, in_hbm(travel), in_hbm(tiles),
        scratch=(
            compact, compact, pltpu.VMEM((LANES, LANES), F32), indices, indices,
            pltpu.VMEM(travel.shape, F32), codes, pltpu.SMEM((z.n_vox,), jnp.int32),
            pltpu.SemaphoreType.DMA((z.slots // GROUP,)), pltpu.SemaphoreType.DMA((3,)), one_sem,
        ),
    )
    n, m = z.data_rows * z.peers, z.segs * VBD
    back, y1, onehot, onehot_t = call(
        owner_first_kernel, "owner1", [VMEM],
        (message, owned, jax.ShapeDtypeStruct((m, n), BF16), jax.ShapeDtypeStruct((n, m), BF16)),
        (VMEM,) * 4, exchange(msg),
    )
    msg, scal1, wide = middle(exchange(back), wide, False)
    back, y2 = call(
        owner_next_kernel, "owner2", [VMEM] * 5, (message, owned), (VMEM,) * 2,
        exchange(msg), onehot, onehot_t, scal1, y1,
    )
    msg, scal2 = middle(exchange(back), wide, True)
    share, back = call(
        owner_last_kernel, "owner3", [VMEM] * 6, (f32(3 * VBD, LANES), f32(z.peers, LANES)),
        (VMEM,) * 2, exchange(msg), onehot, scal1, scal2, y1, y2,
    )
    shares = [share]
    hop = 1
    while hop < n_ray:
        pairs = [(r, r ^ hop) for r in range(n_ray)]
        shares = shares + [lax.ppermute(s, "ray", pairs) for s in shares]
        hop *= 2
    return call(
        final_kernel, "final", [VMEM] * (1 + n_ray), (owned, owned), (VMEM,) * 2,
        exchange(back), *shares,
    )


def solution(mesh):
    return jax.shard_map(
        on_device,
        mesh=mesh,
        in_specs=(
            P(("ray", "vox"), None, None),
            P(("ray", "vox")),
            P(("ray", "vox")),
            P(("ray", "vox")),
            P(("ray", "vox"), None),
        ),
        out_specs=(P("vox", None), P("vox", None)),
        check_vma=False,
    )
```

```python
import functools

import jax
import jax.numpy as jnp
from jax import lax
from jax.experimental import pallas as pl
from jax.experimental.pallas import tpu as pltpu
from jax.sharding import PartitionSpec as P

VBD = 64
LANES = 128
GROUP = 16
F32 = jnp.float32
BF16 = jnp.bfloat16


class Sizes:
    def __init__(self, n_ray, n_vox, slots, ray_blocks):
        self.n_ray, self.n_vox, self.slots, self.ray_blocks = n_ray, n_vox, slots, ray_blocks
        self.peers = n_ray * n_vox
        self.cap = 2 * slots // n_vox
        self.seg = LANES // n_ray
        self.data_rows = max(1, self.cap * self.seg // LANES)
        self.segs = self.cap // self.data_rows
        self.rows = self.data_rows + 1
        self.compact = self.cap * n_vox


def lane(shape):
    return lax.broadcasted_iota(jnp.int32, shape, len(shape) - 1)


def total(x):
    return jnp.sum(jnp.sum(x, axis=1, keepdims=True), axis=0, keepdims=True)


def pick(row, k):
    return jnp.sum(jnp.where(lane(row.shape) == k, row, 0.0), axis=1, keepdims=True)


def shift_lanes(x, amount):
    amount = amount % LANES
    return x if amount == 0 else pltpu.roll(x, amount, axis=1)


def split3(x):
    hi = x.astype(BF16)
    rest = x - hi.astype(F32)
    mid = rest.astype(BF16)
    low = (rest - mid.astype(F32)).astype(BF16)
    return jnp.concatenate([hi, mid, low], axis=1)


def select_dot(onehot, x):
    width = x.shape[1]
    out = jnp.dot(onehot, split3(x), preferred_element_type=F32)
    return out[:, :width] + out[:, width : 2 * width] + out[:, 2 * width :]


def tile_copy(tiles_hbm, tiles_v, sem, c):
    part = pl.ds(c * GROUP, GROUP)
    return pltpu.make_async_copy(tiles_hbm.at[part], tiles_v.at[part], sem.at[c])


def write_products(z, prod, msg, meta):
    segment = lane((z.n_vox, LANES)) // z.seg
    for q in range(z.data_rows):
        part = [
            prod[pl.ds((q * z.segs + g) * z.n_vox, z.n_vox), :] for g in range(z.segs)
        ]
        for r in range(z.n_ray):
            out = jnp.zeros((z.n_vox, LANES), F32)
            for g in range(z.segs):
                out = jnp.where(segment == g, shift_lanes(part[g], (g - r) * z.seg), out)
            msg[pl.ds(r * z.n_vox * z.rows + q, z.n_vox, stride=z.rows), :] = out
    for r in range(z.n_ray):
        msg[pl.ds(r * z.n_vox * z.rows + z.data_rows, z.n_vox, stride=z.rows), :] = jnp.where(
            lane((z.n_vox, LANES)) == z.cap + 1, jnp.float32(r), meta
        )


def backward(groups, where_of, tiles_v, wide, prod, ready=None):
    def step(c, carry):
        if ready is not None:
            ready(c)
        for s in range(GROUP):
            t = c * GROUP + s
            ray, row = where_of(t)
            prod[pl.ds(row, 1), :] = jnp.sum(tiles_v[t] * wide[ray], axis=0, keepdims=True)
        return carry

    lax.fori_loop(0, groups, step, 0)


def first_kernel(
    z, ray_hbm, vox_hbm, tile_count, travel_hbm, tiles_hbm, msg, wide, code_out, tiles_v,
    prod, named, pad, tile_ray, tile_vox, travel, code, count, sem, small_sem, code_sem,
):
    small = [
        pltpu.make_async_copy(src, dst, small_sem.at[i])
        for i, (src, dst) in enumerate(
            [(travel_hbm, travel), (ray_hbm, tile_ray), (vox_hbm, tile_vox)]
        )
    ]
    live = tile_count[0]
    groups = lax.shift_right_logical(live + (GROUP - 1), GROUP.bit_length() - 1)
    for copy in small:
        copy.start()
    for c in range(z.slots // GROUP):

        @pl.when(c < groups)
        def _():
            tile_copy(tiles_hbm, tiles_v, sem, c).start()

    for o in range(z.n_vox):
        count[o] = 0
    prod[...] = jnp.zeros_like(prod)
    named[...] = jnp.full_like(named, -1.0)
    pad[...] = jnp.zeros_like(pad)
    small[0].wait()
    pad[pl.ds(0, z.ray_blocks), :] = travel[...]
    by_col = pad[...].T
    for r in range(z.ray_blocks):
        wide[r] = jnp.broadcast_to(by_col[:, r : r + 1], (LANES, LANES))
    for copy in small[1:]:
        copy.wait()

    def ready(c):
        tile_copy(tiles_hbm, tiles_v, sem, c).wait()

    def where_of(t):
        vox, ray = tile_vox[t], tile_ray[t]
        owner = lax.shift_right_logical(vox, VBD.bit_length() - 1)
        k = count[owner]
        count[owner] = k + 1
        row = k * z.n_vox + owner
        code[t] = row * 256 + ray
        block = jnp.where(t < live, vox & (VBD - 1), -1).astype(F32)
        named[pl.ds(row, 1), :] = jnp.full((1, LANES), block, F32)
        return ray, row

    code[z.slots] = groups
    backward(groups, where_of, tiles_v, wide, prod, ready)
    keep = pltpu.make_async_copy(code, code_out, code_sem)
    keep.start()
    here = lane((z.n_vox, LANES))
    meta = jnp.where(here == z.cap, total(travel[...] * travel[...]), 0.0)
    for k in range(z.cap):
        meta = jnp.where(here == k, named[pl.ds(k * z.n_vox, z.n_vox), :], meta)
    write_products(z, prod, msg, meta)
    keep.wait()


def middle_kernel(
    z, code_v, back, old, tiles_v, msg, scal, *refs
):
    wide, prod, vox_rows, sums, sems, code, code_sem = refs
    fetch = pltpu.make_async_copy(code_v, code, code_sem)
    fetch.start()
    meta = back[pl.ds(z.data_rows, z.peers, stride=z.rows), :]
    alpha = jnp.sqrt(pick(jnp.sum(meta, axis=0, keepdims=True), 0))
    beta = pick(meta[0:1], 1)
    here = lane((8, LANES))
    scal[...] = jnp.where(here == 0, alpha, jnp.where(here == 1, beta, 0.0))
    segment = lane((z.n_vox, LANES)) // z.seg
    for q in range(z.data_rows):
        part = [
            back[pl.ds(r * z.n_vox * z.rows + q, z.n_vox, stride=z.rows), :]
            for r in range(z.n_ray)
        ]
        for g in range(z.segs):
            row = jnp.zeros((z.n_vox, LANES), F32)
            for r in range(z.n_ray):
                row = jnp.where(segment == r, shift_lanes(part[r], (r - g) * z.seg), row)
            vox_rows[pl.ds((q * z.segs + g) * z.n_vox, z.n_vox), :] = row / alpha
    lane_share = -alpha / beta * (1.0 / LANES)
    for r in range(z.ray_blocks):
        sums[r] = old[r] * lane_share
        sems[r] = jnp.zeros((LANES, LANES), F32)
    prod[...] = jnp.zeros_like(prod)
    fetch.wait()
    groups = code[z.slots]

    def where_of(t):
        both = code[t]
        return both & 255, lax.shift_right_logical(both, 8)

    def step(c, carry):
        for s in range(GROUP):
            t = c * GROUP + s
            ray, row = where_of(t)
            into = sums if s % 2 == 0 else sems
            into[ray] += tiles_v[t] * vox_rows[pl.ds(row, 1), :]
        return carry

    lax.fori_loop(0, groups, step, 0)
    square = jnp.zeros((LANES, LANES), F32)
    for r in range(z.ray_blocks):
        u = jnp.broadcast_to(
            jnp.sum(sums[r] + sems[r], axis=1, keepdims=True), (LANES, LANES)
        )
        wide[r] = u
        square += u * u
    backward(groups, where_of, tiles_v, wide, prod)
    meta = jnp.where(
        lane((z.n_vox, LANES)) == z.cap, total(square) * (1.0 / LANES), 0.0
    )
    write_products(z, prod, msg, meta)


def one_hots(z, meta, onehot, onehot_t):
    wide = jnp.concatenate(
        [shift_lanes(meta, -q * z.segs) for q in range(z.data_rows)], axis=0
    )
    n = z.data_rows * z.peers
    tall = wide.T
    block = lax.broadcasted_iota(jnp.int32, (VBD, n), 0).astype(F32)
    for g in range(z.segs):
        onehot[pl.ds(g * VBD, VBD), :] = (tall[g : g + 1, :] == block).astype(F32).astype(BF16)
    here = lane((n, LANES))
    local = (here % VBD).astype(F32)
    per = LANES // VBD
    for h in range(z.segs // per):
        named = wide[:, h * per : h * per + 1]
        for e in range(1, per):
            named = jnp.where(here // VBD == e, wide[:, h * per + e : h * per + e + 1], named)
        onehot_t[:, pl.ds(h * LANES, LANES)] = (named == local).astype(F32).astype(BF16)


def own_sum(z, msg, onehot):
    data = jnp.concatenate(
        [msg[pl.ds(q, z.peers, stride=z.rows), :] for q in range(z.data_rows)], axis=0
    )
    part = select_dot(onehot[...], data)
    segment = lane((VBD, LANES)) // z.seg
    out = jnp.zeros((VBD, LANES), F32)
    for g in range(z.segs):
        out = jnp.where(segment == g, part[g * VBD : (g + 1) * VBD], out)
    step = LANES // 2
    while step >= z.seg:
        out = out + shift_lanes(out, step)
        step //= 2
    return out


def give_back(z, y, onehot_t, beta, back):
    segment = lane((VBD, LANES)) // z.seg
    square = total(jnp.where(segment == 0, y * y, 0.0))
    spread = jnp.concatenate(
        [jnp.where(segment == g, y, 0.0) for g in range(z.segs)], axis=0
    )
    data = select_dot(onehot_t[...], spread)
    for q in range(z.data_rows):
        back[pl.ds(q, z.peers, stride=z.rows), :] = data[q * z.peers : (q + 1) * z.peers]
    here = lane((z.peers, LANES))
    back[pl.ds(z.data_rows, z.peers, stride=z.rows), :] = jnp.where(
        here == 0, square, jnp.where(here == 1, beta, 0.0)
    )


def message_beta(z, msg):
    meta = msg[pl.ds(z.data_rows, z.peers, stride=z.rows), :]
    return meta, jnp.sqrt(pick(jnp.sum(meta, axis=0, keepdims=True), z.cap))


def owner_first_kernel(z, msg, back, y_out, onehot, onehot_t):
    meta, beta = message_beta(z, msg)
    one_hots(z, meta, onehot, onehot_t)
    y = own_sum(z, msg, onehot) / beta
    y_out[...] = y
    give_back(z, y, onehot_t, beta, back)


def owner_next_kernel(z, msg, onehot, onehot_t, scal, y_in, back, y_out):
    _, beta = message_beta(z, msg)
    alpha = scal[0:1, 0:1]
    y = own_sum(z, msg, onehot) / beta - beta * (y_in[...] / alpha)
    y_out[...] = y
    give_back(z, y, onehot_t, beta, back)


def owner_last_kernel(z, msg, onehot, scal1, scal2, y1, y2, share, back):
    meta, beta3 = message_beta(z, msg)
    mine = pick(meta[0:1], z.cap + 1)
    alpha1, beta1 = scal1[0:1, 0:1], scal1[0:1, 1:2]
    alpha2, beta2 = scal2[0:1, 0:1], scal2[0:1, 1:2]
    v1, v2 = y1[...] / alpha1, y2[...] / alpha2
    w = own_sum(z, msg, onehot) / beta3 - beta3 * v2
    rho1 = jnp.sqrt(alpha1 * alpha1 + beta2 * beta2)
    c1, s1 = alpha1 / rho1, beta2 / rho1
    solution = c1 * beta1 / rho1 * v1
    direction = v2 - s1 * alpha2 / rho1 * v1
    rhobar, phibar = -c1 * alpha2, s1 * beta1
    rho2 = jnp.sqrt(rhobar * rhobar + beta3 * beta3)
    solution = solution + (rhobar / rho2) * phibar / rho2 * direction
    segment = lane((VBD, LANES)) // z.seg
    keep = segment.astype(F32) == mine
    share[pl.ds(0, VBD), :] = jnp.where(keep, w, 0.0)
    share[pl.ds(VBD, VBD), :] = jnp.where(keep, solution, 0.0)
    share[pl.ds(2 * VBD, VBD), :] = jnp.where(keep, direction, 0.0)
    here = lane((z.peers, LANES))
    square = total(jnp.where(segment == 0, w * w, 0.0))
    back[...] = jnp.where(
        here == 0, square, jnp.where(here == 1, beta3 / rho2 / rho2, 0.0)
    )


def final_kernel(z, back, *refs):
    shares, solution, direction = refs[:-2], refs[-2], refs[-1]
    whole = shares[0][...]
    for share in shares[1:]:
        whole = whole + share[...]
    alpha = jnp.sqrt(pick(jnp.sum(back[...], axis=0, keepdims=True), 0))
    factor = pick(back[0:1, :], 1) * alpha
    solution[...] = whole[VBD : 2 * VBD]
    direction[...] = whole[:VBD] / alpha - factor * whole[2 * VBD :]


SMEM = pl.BlockSpec(memory_space=pltpu.SMEM)
VMEM = pl.BlockSpec(memory_space=pltpu.VMEM)
HBM = pl.BlockSpec(memory_space=pltpu.HBM)
PARAMS = pltpu.CompilerParams(vmem_limit_bytes=24 * 1024 * 1024)


def in_hbm(x):
    return pltpu.with_memory_space_constraint(x, pltpu.HBM)


def f32(*shape):
    return jax.ShapeDtypeStruct(shape, F32)


def on_device(tiles, tile_ray, tile_vox, tile_count, travel):
    n_ray, n_vox = lax.axis_size("ray"), lax.axis_size("vox")
    z = Sizes(n_ray, n_vox, tiles.shape[0], travel.shape[0])
    message = f32(z.peers * z.rows, LANES)
    wide_rays = f32(z.ray_blocks, LANES, LANES)
    owned = f32(VBD, LANES)

    def call(kernel, name, in_specs, out_shape, out_specs, *args, scratch=()):
        return pl.pallas_call(
            functools.partial(kernel, z), name=name, in_specs=in_specs, out_shape=out_shape,
            out_specs=out_specs, scratch_shapes=scratch, compiler_params=PARAMS,
        )(*args)

    def exchange(x):
        n = x.shape[0]
        out = lax.all_to_all(x.reshape(n, 1, LANES), ("ray", "vox"), 0, 0, tiled=True)
        return out.reshape(n, LANES)

    per_ray = pltpu.VMEM((z.ray_blocks, LANES, LANES), F32)
    compact = pltpu.VMEM((z.compact, LANES), F32)
    indices = pltpu.SMEM((z.slots,), jnp.int32)
    codes = pltpu.SMEM((z.slots + 1,), jnp.int32)
    one_sem = pltpu.SemaphoreType.DMA(())

    def middle(back, wide, last):
        scratch = (compact, compact, per_ray, per_ray, codes, one_sem)
        out = (message, f32(8, LANES))
        return call(
            middle_kernel, "middle2" if last else "middle1", (VMEM,) * 4,
            out if last else out + (wide_rays,), (VMEM,) * (2 if last else 3),
            code, back, wide, tiles_v, scratch=(per_ray,) + scratch if last else scratch,
        )

    msg, wide, code, tiles_v = call(
        first_kernel, "first", [HBM, HBM, SMEM, HBM, HBM],
        (message, wide_rays, jax.ShapeDtypeStruct((z.slots + 1,), jnp.int32), f32(*tiles.shape)),
        (VMEM,) * 4,
        in_hbm(tile_ray), in_hbm(tile_vox), tile_count, in_hbm(travel), in_hbm(tiles),
        scratch=(
            compact, compact, pltpu.VMEM((LANES, LANES), F32), indices, indices,
            pltpu.VMEM(travel.shape, F32), codes, pltpu.SMEM((z.n_vox,), jnp.int32),
            pltpu.SemaphoreType.DMA((z.slots // GROUP,)), pltpu.SemaphoreType.DMA((3,)), one_sem,
        ),
    )
    n, m = z.data_rows * z.peers, z.segs * VBD
    back, y1, onehot, onehot_t = call(
        owner_first_kernel, "owner1", [VMEM],
        (message, owned, jax.ShapeDtypeStruct((m, n), BF16), jax.ShapeDtypeStruct((n, m), BF16)),
        (VMEM,) * 4, exchange(msg),
    )
    msg, scal1, wide = middle(exchange(back), wide, False)
    back, y2 = call(
        owner_next_kernel, "owner2", [VMEM] * 5, (message, owned), (VMEM,) * 2,
        exchange(msg), onehot, onehot_t, scal1, y1,
    )
    msg, scal2 = middle(exchange(back), wide, True)
    share, back = call(
        owner_last_kernel, "owner3", [VMEM] * 6, (f32(3 * VBD, LANES), f32(z.peers, LANES)),
        (VMEM,) * 2, exchange(msg), onehot, scal1, scal2, y1, y2,
    )
    shares = [share] + [
        lax.ppermute(share, "ray", [(r, r ^ hop) for r in range(n_ray)]) for hop in range(1, n_ray)
    ]
    return call(
        final_kernel, "final", [VMEM] * (1 + n_ray), (owned, owned), (VMEM,) * 2,
        exchange(back), *shares,
    )


def solution(mesh):
    return jax.shard_map(
        on_device,
        mesh=mesh,
        in_specs=(
            P(("ray", "vox"), None, None),
            P(("ray", "vox")),
            P(("ray", "vox")),
            P(("ray", "vox")),
            P(("ray", "vox"), None),
        ),
        out_specs=(P("vox", None), P("vox", None)),
        check_vma=False,
    )
```

```python
import functools

import jax
import jax.numpy as jnp
from jax import lax
from jax.experimental import pallas as pl
from jax.experimental.pallas import tpu as pltpu
from jax.sharding import PartitionSpec as P

VBD = 64
LANES = 128
GROUP = 16
F32 = jnp.float32
BF16 = jnp.bfloat16


class Sizes:
    def __init__(self, n_ray, n_vox, slots, ray_blocks):
        self.n_ray, self.n_vox, self.slots, self.ray_blocks = n_ray, n_vox, slots, ray_blocks
        self.peers = n_ray * n_vox
        self.cap = 2 * slots // n_vox
        self.seg = LANES // n_ray
        self.data_rows = max(1, self.cap * self.seg // LANES)
        self.segs = self.cap // self.data_rows
        self.rows = self.data_rows + 1
        self.compact = self.cap * n_vox


def lane(shape):
    return lax.broadcasted_iota(jnp.int32, shape, len(shape) - 1)


def total(x):
    return jnp.sum(jnp.sum(x, axis=1, keepdims=True), axis=0, keepdims=True)


def pick(row, k):
    return jnp.sum(jnp.where(lane(row.shape) == k, row, 0.0), axis=1, keepdims=True)


def shift_lanes(x, amount):
    amount = amount % LANES
    return x if amount == 0 else pltpu.roll(x, amount, axis=1)


def split3(x):
    hi = x.astype(BF16)
    rest = x - hi.astype(F32)
    mid = rest.astype(BF16)
    low = (rest - mid.astype(F32)).astype(BF16)
    return jnp.concatenate([hi, mid, low], axis=1)


def select_dot(onehot, x):
    width = x.shape[1]
    out = jnp.dot(onehot, split3(x), preferred_element_type=F32)
    return out[:, :width] + out[:, width : 2 * width] + out[:, 2 * width :]


def tile_copy(tiles_hbm, tiles_v, sem, c):
    part = pl.ds(c * GROUP, GROUP)
    return pltpu.make_async_copy(tiles_hbm.at[part], tiles_v.at[part], sem.at[c])


def write_products(z, prod, msg, meta):
    segment = lane((z.n_vox, LANES)) // z.seg
    for q in range(z.data_rows):
        part = [
            prod[pl.ds((q * z.segs + g) * z.n_vox, z.n_vox), :] for g in range(z.segs)
        ]
        for r in range(z.n_ray):
            out = jnp.zeros((z.n_vox, LANES), F32)
            for g in range(z.segs):
                out = jnp.where(segment == g, shift_lanes(part[g], (g - r) * z.seg), out)
            msg[pl.ds(r * z.n_vox * z.rows + q, z.n_vox, stride=z.rows), :] = out
    for r in range(z.n_ray):
        msg[pl.ds(r * z.n_vox * z.rows + z.data_rows, z.n_vox, stride=z.rows), :] = jnp.where(
            lane((z.n_vox, LANES)) == z.cap + 1, jnp.float32(r), meta
        )


def backward(groups, where_of, tiles_v, wide, prod, ready=None):
    def step(c, carry):
        if ready is not None:
            ready(c)
        for s in range(GROUP):
            t = c * GROUP + s
            ray, row = where_of(t)
            prod[pl.ds(row, 1), :] = jnp.sum(tiles_v[t] * wide[ray], axis=0, keepdims=True)
        return carry

    lax.fori_loop(0, groups, step, 0)


def first_kernel(
    z, ray_hbm, vox_hbm, tile_count, travel_hbm, tiles_hbm, msg, wide, code, tiles_v,
    prod, named, pad, tile_ray, tile_vox, travel, count, sem, small_sem,
):
    small = [
        pltpu.make_async_copy(src, dst, small_sem.at[i])
        for i, (src, dst) in enumerate(
            [(travel_hbm, travel), (ray_hbm, tile_ray), (vox_hbm, tile_vox)]
        )
    ]
    live = tile_count[0]
    groups = lax.shift_right_logical(live + (GROUP - 1), GROUP.bit_length() - 1)
    for copy in small:
        copy.start()
    for c in range(z.slots // GROUP):

        @pl.when(c < groups)
        def _():
            tile_copy(tiles_hbm, tiles_v, sem, c).start()

    for o in range(z.n_vox):
        count[o] = 0
    prod[...] = jnp.zeros_like(prod)
    named[...] = jnp.full_like(named, -1.0)
    code[...] = jnp.zeros_like(code)
    pad[...] = jnp.zeros_like(pad)
    small[0].wait()
    pad[pl.ds(0, z.ray_blocks), :] = travel[...]
    by_col = pad[...].T
    for r in range(z.ray_blocks):
        wide[r] = jnp.broadcast_to(by_col[:, r : r + 1], (LANES, LANES))
    for copy in small[1:]:
        copy.wait()

    def ready(c):
        tile_copy(tiles_hbm, tiles_v, sem, c).wait()

    def where_of(t):
        vox, ray = tile_vox[t], tile_ray[t]
        owner = lax.shift_right_logical(vox, VBD.bit_length() - 1)
        k = count[owner]
        count[owner] = k + 1
        row = k * z.n_vox + owner
        code[pl.ds(t, 1), :] = jnp.full((1, LANES), row * 256 + ray, jnp.int32)
        block = jnp.where(t < live, vox & (VBD - 1), -1).astype(F32)
        named[pl.ds(row, 1), :] = jnp.full((1, LANES), block, F32)
        return ray, row

    code[pl.ds(z.slots, 1), :] = jnp.full((1, LANES), groups, jnp.int32)
    backward(groups, where_of, tiles_v, wide, prod, ready)
    here = lane((z.n_vox, LANES))
    meta = jnp.where(here == z.cap, total(travel[...] * travel[...]), 0.0)
    for k in range(z.cap):
        meta = jnp.where(here == k, named[pl.ds(k * z.n_vox, z.n_vox), :], meta)
    write_products(z, prod, msg, meta)


def middle_kernel(
    z, code_v, back, old, tiles_v, msg, scal, *refs
):
    wide, prod, vox_rows, sums, sems, code = refs
    for t in range(z.slots + 1):
        code[t] = code_v[t, 0]
    meta = back[pl.ds(z.data_rows, z.peers, stride=z.rows), :]
    alpha = jnp.sqrt(pick(jnp.sum(meta, axis=0, keepdims=True), 0))
    beta = pick(meta[0:1], 1)
    here = lane((8, LANES))
    scal[...] = jnp.where(here == 0, alpha, jnp.where(here == 1, beta, 0.0))
    segment = lane((z.n_vox, LANES)) // z.seg
    for q in range(z.data_rows):
        part = [
            back[pl.ds(r * z.n_vox * z.rows + q, z.n_vox, stride=z.rows), :]
            for r in range(z.n_ray)
        ]
        for g in range(z.segs):
            row = jnp.zeros((z.n_vox, LANES), F32)
            for r in range(z.n_ray):
                row = jnp.where(segment == r, shift_lanes(part[r], (r - g) * z.seg), row)
            vox_rows[pl.ds((q * z.segs + g) * z.n_vox, z.n_vox), :] = row / alpha
    lane_share = -alpha / beta * (1.0 / LANES)
    for r in range(z.ray_blocks):
        sums[r] = old[r] * lane_share
        sems[r] = jnp.zeros((LANES, LANES), F32)
    prod[...] = jnp.zeros_like(prod)
    groups = code[z.slots]

    def where_of(t):
        both = code[t]
        return both & 255, lax.shift_right_logical(both, 8)

    def step(c, carry):
        for s in range(GROUP):
            t = c * GROUP + s
            ray, row = where_of(t)
            into = sums if s % 2 == 0 else sems
            into[ray] += tiles_v[t] * vox_rows[pl.ds(row, 1), :]
        return carry

    lax.fori_loop(0, groups, step, 0)
    square = jnp.zeros((LANES, LANES), F32)
    for r in range(z.ray_blocks):
        u = jnp.broadcast_to(
            jnp.sum(sums[r] + sems[r], axis=1, keepdims=True), (LANES, LANES)
        )
        wide[r] = u
        square += u * u
    backward(groups, where_of, tiles_v, wide, prod)
    meta = jnp.where(
        lane((z.n_vox, LANES)) == z.cap, total(square) * (1.0 / LANES), 0.0
    )
    write_products(z, prod, msg, meta)


def one_hots(z, meta, onehot, onehot_t):
    wide = jnp.concatenate(
        [shift_lanes(meta, -q * z.segs) for q in range(z.data_rows)], axis=0
    )
    n = z.data_rows * z.peers
    tall = wide.T
    block = lax.broadcasted_iota(jnp.int32, (VBD, n), 0).astype(F32)
    for g in range(z.segs):
        onehot[pl.ds(g * VBD, VBD), :] = (tall[g : g + 1, :] == block).astype(F32).astype(BF16)
    here = lane((n, LANES))
    local = (here % VBD).astype(F32)
    per = LANES // VBD
    for h in range(z.segs // per):
        named = wide[:, h * per : h * per + 1]
        for e in range(1, per):
            named = jnp.where(here // VBD == e, wide[:, h * per + e : h * per + e + 1], named)
        onehot_t[:, pl.ds(h * LANES, LANES)] = (named == local).astype(F32).astype(BF16)


def own_sum(z, msg, onehot):
    data = jnp.concatenate(
        [msg[pl.ds(q, z.peers, stride=z.rows), :] for q in range(z.data_rows)], axis=0
    )
    part = select_dot(onehot[...], data)
    segment = lane((VBD, LANES)) // z.seg
    out = jnp.zeros((VBD, LANES), F32)
    for g in range(z.segs):
        out = jnp.where(segment == g, part[g * VBD : (g + 1) * VBD], out)
    step = LANES // 2
    while step >= z.seg:
        out = out + shift_lanes(out, step)
        step //= 2
    return out


def give_back(z, y, onehot_t, beta, back):
    segment = lane((VBD, LANES)) // z.seg
    square = total(jnp.where(segment == 0, y * y, 0.0))
    spread = jnp.concatenate(
        [jnp.where(segment == g, y, 0.0) for g in range(z.segs)], axis=0
    )
    data = select_dot(onehot_t[...], spread)
    for q in range(z.data_rows):
        back[pl.ds(q, z.peers, stride=z.rows), :] = data[q * z.peers : (q + 1) * z.peers]
    here = lane((z.peers, LANES))
    back[pl.ds(z.data_rows, z.peers, stride=z.rows), :] = jnp.where(
        here == 0, square, jnp.where(here == 1, beta, 0.0)
    )


def message_beta(z, msg):
    meta = msg[pl.ds(z.data_rows, z.peers, stride=z.rows), :]
    return meta, jnp.sqrt(pick(jnp.sum(meta, axis=0, keepdims=True), z.cap))


def owner_first_kernel(z, msg, back, y_out, onehot, onehot_t):
    meta, beta = message_beta(z, msg)
    one_hots(z, meta, onehot, onehot_t)
    y = own_sum(z, msg, onehot) / beta
    y_out[...] = y
    give_back(z, y, onehot_t, beta, back)


def owner_next_kernel(z, msg, onehot, onehot_t, scal, y_in, back, y_out):
    _, beta = message_beta(z, msg)
    alpha = scal[0:1, 0:1]
    y = own_sum(z, msg, onehot) / beta - beta * (y_in[...] / alpha)
    y_out[...] = y
    give_back(z, y, onehot_t, beta, back)


def owner_last_kernel(z, msg, onehot, scal1, scal2, y1, y2, share, back):
    meta, beta3 = message_beta(z, msg)
    mine = pick(meta[0:1], z.cap + 1)
    alpha1, beta1 = scal1[0:1, 0:1], scal1[0:1, 1:2]
    alpha2, beta2 = scal2[0:1, 0:1], scal2[0:1, 1:2]
    v1, v2 = y1[...] / alpha1, y2[...] / alpha2
    w = own_sum(z, msg, onehot) / beta3 - beta3 * v2
    rho1 = jnp.sqrt(alpha1 * alpha1 + beta2 * beta2)
    c1, s1 = alpha1 / rho1, beta2 / rho1
    solution = c1 * beta1 / rho1 * v1
    direction = v2 - s1 * alpha2 / rho1 * v1
    rhobar, phibar = -c1 * alpha2, s1 * beta1
    rho2 = jnp.sqrt(rhobar * rhobar + beta3 * beta3)
    solution = solution + (rhobar / rho2) * phibar / rho2 * direction
    segment = lane((VBD, LANES)) // z.seg
    keep = segment.astype(F32) == mine
    share[pl.ds(0, VBD), :] = jnp.where(keep, w, 0.0)
    share[pl.ds(VBD, VBD), :] = jnp.where(keep, solution, 0.0)
    share[pl.ds(2 * VBD, VBD), :] = jnp.where(keep, direction, 0.0)
    here = lane((z.peers, LANES))
    square = total(jnp.where(segment == 0, w * w, 0.0))
    back[...] = jnp.where(
        here == 0, square, jnp.where(here == 1, beta3 / rho2 / rho2, 0.0)
    )


def final_kernel(z, back, *refs):
    shares, solution, direction = refs[:-2], refs[-2], refs[-1]
    whole = shares[0][...]
    for share in shares[1:]:
        whole = whole + share[...]
    alpha = jnp.sqrt(pick(jnp.sum(back[...], axis=0, keepdims=True), 0))
    factor = pick(back[0:1, :], 1) * alpha
    solution[...] = whole[VBD : 2 * VBD]
    direction[...] = whole[:VBD] / alpha - factor * whole[2 * VBD :]


SMEM = pl.BlockSpec(memory_space=pltpu.SMEM)
VMEM = pl.BlockSpec(memory_space=pltpu.VMEM)
HBM = pl.BlockSpec(memory_space=pltpu.HBM)
PARAMS = pltpu.CompilerParams(vmem_limit_bytes=24 * 1024 * 1024)


def in_hbm(x):
    return pltpu.with_memory_space_constraint(x, pltpu.HBM)


def f32(*shape):
    return jax.ShapeDtypeStruct(shape, F32)


def on_device(tiles, tile_ray, tile_vox, tile_count, travel):
    n_ray, n_vox = lax.axis_size("ray"), lax.axis_size("vox")
    z = Sizes(n_ray, n_vox, tiles.shape[0], travel.shape[0])
    message = f32(z.peers * z.rows, LANES)
    wide_rays = f32(z.ray_blocks, LANES, LANES)
    owned = f32(VBD, LANES)

    def call(kernel, name, in_specs, out_shape, out_specs, *args, scratch=()):
        return pl.pallas_call(
            functools.partial(kernel, z), name=name, in_specs=in_specs, out_shape=out_shape,
            out_specs=out_specs, scratch_shapes=scratch, compiler_params=PARAMS,
        )(*args)

    def exchange(x):
        n = x.shape[0]
        out = lax.all_to_all(x.reshape(n, 1, LANES), ("ray", "vox"), 0, 0, tiled=True)
        return out.reshape(n, LANES)

    per_ray = pltpu.VMEM((z.ray_blocks, LANES, LANES), F32)
    compact = pltpu.VMEM((z.compact, LANES), F32)
    indices = pltpu.SMEM((z.slots,), jnp.int32)

    codes = pltpu.SMEM((z.slots + 1,), jnp.int32)

    def middle(back, wide, last):
        scratch = (compact, compact, per_ray, per_ray, codes)
        out = (message, f32(8, LANES))
        return call(
            middle_kernel, "middle2" if last else "middle1", (VMEM,) * 4,
            out if last else out + (wide_rays,), (VMEM,) * (2 if last else 3),
            code, back, wide, tiles_v, scratch=(per_ray,) + scratch if last else scratch,
        )

    msg, wide, code, tiles_v = call(
        first_kernel, "first", [HBM, HBM, SMEM, HBM, HBM],
        (message, wide_rays, jax.ShapeDtypeStruct((z.slots + 8, LANES), jnp.int32), f32(*tiles.shape)),
        (VMEM,) * 4,
        in_hbm(tile_ray), in_hbm(tile_vox), tile_count, in_hbm(travel), in_hbm(tiles),
        scratch=(
            compact, compact, pltpu.VMEM((LANES, LANES), F32), indices, indices,
            pltpu.VMEM(travel.shape, F32), pltpu.SMEM((z.n_vox,), jnp.int32),
            pltpu.SemaphoreType.DMA((z.slots // GROUP,)), pltpu.SemaphoreType.DMA((3,)),
        ),
    )
    n, m = z.data_rows * z.peers, z.segs * VBD
    back, y1, onehot, onehot_t = call(
        owner_first_kernel, "owner1", [VMEM],
        (message, owned, jax.ShapeDtypeStruct((m, n), BF16), jax.ShapeDtypeStruct((n, m), BF16)),
        (VMEM,) * 4, exchange(msg),
    )
    msg, scal1, wide = middle(exchange(back), wide, False)
    back, y2 = call(
        owner_next_kernel, "owner2", [VMEM] * 5, (message, owned), (VMEM,) * 2,
        exchange(msg), onehot, onehot_t, scal1, y1,
    )
    msg, scal2 = middle(exchange(back), wide, True)
    share, back = call(
        owner_last_kernel, "owner3", [VMEM] * 6, (f32(3 * VBD, LANES), f32(z.peers, LANES)),
        (VMEM,) * 2, exchange(msg), onehot, scal1, scal2, y1, y2,
    )
    shares = [share] + [
        lax.ppermute(share, "ray", [(r, r ^ hop) for r in range(n_ray)]) for hop in range(1, n_ray)
    ]
    return call(
        final_kernel, "final", [VMEM] * (1 + n_ray), (owned, owned), (VMEM,) * 2,
        exchange(back), *shares,
    )


def solution(mesh):
    return jax.shard_map(
        on_device,
        mesh=mesh,
        in_specs=(
            P(("ray", "vox"), None, None),
            P(("ray", "vox")),
            P(("ray", "vox")),
            P(("ray", "vox")),
            P(("ray", "vox"), None),
        ),
        out_specs=(P("vox", None), P("vox", None)),
        check_vma=False,
    )
```

```python
import functools

import jax
import jax.numpy as jnp
from jax import lax
from jax.experimental import pallas as pl
from jax.experimental.pallas import tpu as pltpu
from jax.sharding import PartitionSpec as P

VBD = 64
LANES = 128
GROUP = 16
F32 = jnp.float32
BF16 = jnp.bfloat16


class Sizes:
    def __init__(self, n_ray, n_vox, slots, ray_blocks):
        self.n_ray, self.n_vox, self.slots, self.ray_blocks = n_ray, n_vox, slots, ray_blocks
        self.peers = n_ray * n_vox
        self.cap = 2 * slots // n_vox
        self.seg = LANES // n_ray
        self.data_rows = max(1, self.cap * self.seg // LANES)
        self.segs = self.cap // self.data_rows
        self.rows = self.data_rows + 1
        self.compact = self.cap * n_vox


def lane(shape):
    return lax.broadcasted_iota(jnp.int32, shape, len(shape) - 1)


def total(x):
    return jnp.sum(jnp.sum(x, axis=1, keepdims=True), axis=0, keepdims=True)


def pick(row, k):
    return jnp.sum(jnp.where(lane(row.shape) == k, row, 0.0), axis=1, keepdims=True)


def shift_lanes(x, amount):
    amount = amount % LANES
    return x if amount == 0 else pltpu.roll(x, amount, axis=1)


def split3(x):
    hi = x.astype(BF16)
    rest = x - hi.astype(F32)
    mid = rest.astype(BF16)
    low = (rest - mid.astype(F32)).astype(BF16)
    return jnp.concatenate([hi, mid, low], axis=1)


def select_dot(onehot, x):
    width = x.shape[1]
    out = jnp.dot(onehot, split3(x), preferred_element_type=F32)
    return out[:, :width] + out[:, width : 2 * width] + out[:, 2 * width :]


def tile_copy(tiles_hbm, tiles_v, sem, c):
    part = pl.ds(c * GROUP, GROUP)
    return pltpu.make_async_copy(tiles_hbm.at[part], tiles_v.at[part], sem.at[c])


def write_products(z, prod, msg, meta):
    segment = lane((z.n_vox, LANES)) // z.seg
    for q in range(z.data_rows):
        part = [
            prod[pl.ds((q * z.segs + g) * z.n_vox, z.n_vox), :] for g in range(z.segs)
        ]
        for r in range(z.n_ray):
            out = jnp.zeros((z.n_vox, LANES), F32)
            for g in range(z.segs):
                out = jnp.where(segment == g, shift_lanes(part[g], (g - r) * z.seg), out)
            msg[pl.ds(r * z.n_vox * z.rows + q, z.n_vox, stride=z.rows), :] = out
    for r in range(z.n_ray):
        msg[pl.ds(r * z.n_vox * z.rows + z.data_rows, z.n_vox, stride=z.rows), :] = jnp.where(
            lane((z.n_vox, LANES)) == z.cap + 1, jnp.float32(r), meta
        )


def backward(groups, where_of, tiles_v, wide, prod, ready=None):
    def step(c, carry):
        if ready is not None:
            ready(c)
        for s in range(GROUP):
            t = c * GROUP + s
            ray, row = where_of(t)
            prod[pl.ds(row, 1), :] = jnp.sum(tiles_v[t] * wide[ray], axis=0, keepdims=True)
        return carry

    lax.fori_loop(0, groups, step, 0)


def first_kernel(
    z, ray_hbm, vox_hbm, tile_count, travel_hbm, tiles_hbm, msg, wide, code, tiles_v,
    prod, named, pad, tile_ray, tile_vox, travel, count, sem, small_sem,
):
    small = [
        pltpu.make_async_copy(src, dst, small_sem.at[i])
        for i, (src, dst) in enumerate(
            [(travel_hbm, travel), (ray_hbm, tile_ray), (vox_hbm, tile_vox)]
        )
    ]
    live = tile_count[0]
    groups = lax.shift_right_logical(live + (GROUP - 1), GROUP.bit_length() - 1)
    for copy in small:
        copy.start()
    for c in range(z.slots // GROUP):

        @pl.when(c < groups)
        def _():
            tile_copy(tiles_hbm, tiles_v, sem, c).start()

    for o in range(z.n_vox):
        count[o] = 0
    prod[...] = jnp.zeros_like(prod)
    named[...] = jnp.full_like(named, -1.0)
    code[...] = jnp.zeros_like(code)
    pad[...] = jnp.zeros_like(pad)
    small[0].wait()
    pad[pl.ds(0, z.ray_blocks), :] = travel[...]
    by_col = pad[...].T
    parts = split3(by_col)
    packed = parts[:, :LANES].astype(F32)
    for i in (1, 2):
        packed += shift_lanes(parts[:, i * LANES : (i + 1) * LANES].astype(F32), i * z.ray_blocks)
    packed = packed.astype(BF16)
    from_row = lax.broadcasted_iota(jnp.int32, (LANES, LANES), 0)
    from_row = jnp.where(from_row < 3 * z.ray_blocks, from_row % z.ray_blocks, -1)
    ones = jnp.ones((LANES, LANES), F32)
    for r in range(z.ray_blocks):
        if r % 2:
            from_lane = jnp.where(from_row == r, ones, 0.0).astype(BF16)
            wide[r] = jnp.dot(packed, from_lane, preferred_element_type=F32)
        else:
            wide[r] = jnp.broadcast_to(by_col[:, r : r + 1], (LANES, LANES))
    for copy in small[1:]:
        copy.wait()

    def ready(c):
        tile_copy(tiles_hbm, tiles_v, sem, c).wait()

    def where_of(t):
        vox, ray = tile_vox[t], tile_ray[t]
        owner = lax.shift_right_logical(vox, VBD.bit_length() - 1)
        k = count[owner]
        count[owner] = k + 1
        row = k * z.n_vox + owner
        code[pl.ds(t, 1), :] = jnp.full((1, LANES), row * 256 + ray, jnp.int32)
        block = jnp.where(t < live, vox & (VBD - 1), -1).astype(F32)
        named[pl.ds(row, 1), :] = jnp.full((1, LANES), block, F32)
        return ray, row

    code[pl.ds(z.slots, 1), :] = jnp.full((1, LANES), groups, jnp.int32)
    backward(groups, where_of, tiles_v, wide, prod, ready)
    here = lane((z.n_vox, LANES))
    meta = jnp.where(here == z.cap, total(travel[...] * travel[...]), 0.0)
    for k in range(z.cap):
        meta = jnp.where(here == k, named[pl.ds(k * z.n_vox, z.n_vox), :], meta)
    write_products(z, prod, msg, meta)


def middle_kernel(
    z, code_v, back, old, tiles_v, msg, scal, *refs
):
    wide, prod, vox_rows, sums, sems, code = refs
    for t in range(z.slots + 1):
        code[t] = code_v[t, 0]
    meta = back[pl.ds(z.data_rows, z.peers, stride=z.rows), :]
    alpha = jnp.sqrt(pick(jnp.sum(meta, axis=0, keepdims=True), 0))
    beta = pick(meta[0:1], 1)
    here = lane((8, LANES))
    scal[...] = jnp.where(here == 0, alpha, jnp.where(here == 1, beta, 0.0))
    segment = lane((z.n_vox, LANES)) // z.seg
    for q in range(z.data_rows):
        part = [
            back[pl.ds(r * z.n_vox * z.rows + q, z.n_vox, stride=z.rows), :]
            for r in range(z.n_ray)
        ]
        for g in range(z.segs):
            row = jnp.zeros((z.n_vox, LANES), F32)
            for r in range(z.n_ray):
                row = jnp.where(segment == r, shift_lanes(part[r], (r - g) * z.seg), row)
            vox_rows[pl.ds((q * z.segs + g) * z.n_vox, z.n_vox), :] = row / alpha
    lane_share = -alpha / beta * (1.0 / LANES)
    for r in range(z.ray_blocks):
        sums[r] = old[r] * lane_share
        sems[r] = jnp.zeros((LANES, LANES), F32)
    prod[...] = jnp.zeros_like(prod)
    groups = code[z.slots]

    def where_of(t):
        both = code[t]
        return both & 255, lax.shift_right_logical(both, 8)

    def step(c, carry):
        for s in range(GROUP):
            t = c * GROUP + s
            ray, row = where_of(t)
            into = sums if s % 2 == 0 else sems
            into[ray] += tiles_v[t] * vox_rows[pl.ds(row, 1), :]
        return carry

    lax.fori_loop(0, groups, step, 0)
    square = jnp.zeros((LANES, LANES), F32)
    for r in range(z.ray_blocks):
        both = sums[r] + sems[r]
        if r % 4 == 3:
            ones = jnp.ones((3 * LANES, LANES), BF16)
            u = jnp.dot(split3(both), ones, preferred_element_type=F32)
        else:
            u = jnp.broadcast_to(jnp.sum(both, axis=1, keepdims=True), (LANES, LANES))
        wide[r] = u
        square += u * u
    backward(groups, where_of, tiles_v, wide, prod)
    meta = jnp.where(
        lane((z.n_vox, LANES)) == z.cap, total(square) * (1.0 / LANES), 0.0
    )
    write_products(z, prod, msg, meta)


def one_hots(z, meta, onehot, onehot_t):
    wide = jnp.concatenate(
        [shift_lanes(meta, -q * z.segs) for q in range(z.data_rows)], axis=0
    )
    n = z.data_rows * z.peers
    tall = wide.T
    block = lax.broadcasted_iota(jnp.int32, (VBD, n), 0).astype(F32)
    for g in range(z.segs):
        onehot[pl.ds(g * VBD, VBD), :] = (tall[g : g + 1, :] == block).astype(F32).astype(BF16)
    here = lane((n, LANES))
    local = (here % VBD).astype(F32)
    per = LANES // VBD
    for h in range(z.segs // per):
        named = wide[:, h * per : h * per + 1]
        for e in range(1, per):
            named = jnp.where(here // VBD == e, wide[:, h * per + e : h * per + e + 1], named)
        onehot_t[:, pl.ds(h * LANES, LANES)] = (named == local).astype(F32).astype(BF16)


def own_sum(z, msg, onehot):
    data = jnp.concatenate(
        [msg[pl.ds(q, z.peers, stride=z.rows), :] for q in range(z.data_rows)], axis=0
    )
    part = select_dot(onehot[...], data)
    segment = lane((VBD, LANES)) // z.seg
    out = jnp.zeros((VBD, LANES), F32)
    for g in range(z.segs):
        out = jnp.where(segment == g, part[g * VBD : (g + 1) * VBD], out)
    step = LANES // 2
    while step >= z.seg:
        out = out + shift_lanes(out, step)
        step //= 2
    return out


def give_back(z, y, onehot_t, beta, back):
    segment = lane((VBD, LANES)) // z.seg
    square = total(jnp.where(segment == 0, y * y, 0.0))
    spread = jnp.concatenate(
        [jnp.where(segment == g, y, 0.0) for g in range(z.segs)], axis=0
    )
    data = select_dot(onehot_t[...], spread)
    for q in range(z.data_rows):
        back[pl.ds(q, z.peers, stride=z.rows), :] = data[q * z.peers : (q + 1) * z.peers]
    here = lane((z.peers, LANES))
    back[pl.ds(z.data_rows, z.peers, stride=z.rows), :] = jnp.where(
        here == 0, square, jnp.where(here == 1, beta, 0.0)
    )


def message_beta(z, msg):
    meta = msg[pl.ds(z.data_rows, z.peers, stride=z.rows), :]
    return meta, jnp.sqrt(pick(jnp.sum(meta, axis=0, keepdims=True), z.cap))


def owner_first_kernel(z, msg, back, y_out, onehot, onehot_t):
    meta, beta = message_beta(z, msg)
    one_hots(z, meta, onehot, onehot_t)
    y = own_sum(z, msg, onehot) / beta
    y_out[...] = y
    give_back(z, y, onehot_t, beta, back)


def owner_next_kernel(z, msg, onehot, onehot_t, scal, y_in, back, y_out):
    _, beta = message_beta(z, msg)
    alpha = scal[0:1, 0:1]
    y = own_sum(z, msg, onehot) / beta - beta * (y_in[...] / alpha)
    y_out[...] = y
    give_back(z, y, onehot_t, beta, back)


def owner_last_kernel(z, msg, onehot, scal1, scal2, y1, y2, share, back):
    meta, beta3 = message_beta(z, msg)
    mine = pick(meta[0:1], z.cap + 1)
    alpha1, beta1 = scal1[0:1, 0:1], scal1[0:1, 1:2]
    alpha2, beta2 = scal2[0:1, 0:1], scal2[0:1, 1:2]
    v1, v2 = y1[...] / alpha1, y2[...] / alpha2
    w = own_sum(z, msg, onehot) / beta3 - beta3 * v2
    rho1 = jnp.sqrt(alpha1 * alpha1 + beta2 * beta2)
    c1, s1 = alpha1 / rho1, beta2 / rho1
    solution = c1 * beta1 / rho1 * v1
    direction = v2 - s1 * alpha2 / rho1 * v1
    rhobar, phibar = -c1 * alpha2, s1 * beta1
    rho2 = jnp.sqrt(rhobar * rhobar + beta3 * beta3)
    solution = solution + (rhobar / rho2) * phibar / rho2 * direction
    segment = lane((VBD, LANES)) // z.seg
    keep = segment.astype(F32) == mine
    share[pl.ds(0, VBD), :] = jnp.where(keep, w, 0.0)
    share[pl.ds(VBD, VBD), :] = jnp.where(keep, solution, 0.0)
    share[pl.ds(2 * VBD, VBD), :] = jnp.where(keep, direction, 0.0)
    here = lane((z.peers, LANES))
    square = total(jnp.where(segment == 0, w * w, 0.0))
    back[...] = jnp.where(
        here == 0, square, jnp.where(here == 1, beta3 / rho2 / rho2, 0.0)
    )


def final_kernel(z, back, *refs):
    shares, solution, direction = refs[:-2], refs[-2], refs[-1]
    whole = shares[0][...]
    for share in shares[1:]:
        whole = whole + share[...]
    alpha = jnp.sqrt(pick(jnp.sum(back[...], axis=0, keepdims=True), 0))
    factor = pick(back[0:1, :], 1) * alpha
    solution[...] = whole[VBD : 2 * VBD]
    direction[...] = whole[:VBD] / alpha - factor * whole[2 * VBD :]


SMEM = pl.BlockSpec(memory_space=pltpu.SMEM)
VMEM = pl.BlockSpec(memory_space=pltpu.VMEM)
HBM = pl.BlockSpec(memory_space=pltpu.HBM)
PARAMS = pltpu.CompilerParams(vmem_limit_bytes=24 * 1024 * 1024)


def in_hbm(x):
    return pltpu.with_memory_space_constraint(x, pltpu.HBM)


def f32(*shape):
    return jax.ShapeDtypeStruct(shape, F32)


def on_device(tiles, tile_ray, tile_vox, tile_count, travel):
    n_ray, n_vox = lax.axis_size("ray"), lax.axis_size("vox")
    z = Sizes(n_ray, n_vox, tiles.shape[0], travel.shape[0])
    message = f32(z.peers * z.rows, LANES)
    wide_rays = f32(z.ray_blocks, LANES, LANES)
    owned = f32(VBD, LANES)

    def call(kernel, name, in_specs, out_shape, out_specs, *args, scratch=()):
        return pl.pallas_call(
            functools.partial(kernel, z), name=name, in_specs=in_specs, out_shape=out_shape,
            out_specs=out_specs, scratch_shapes=scratch, compiler_params=PARAMS,
        )(*args)

    def exchange(x):
        n = x.shape[0]
        out = lax.all_to_all(x.reshape(n, 1, LANES), ("ray", "vox"), 0, 0, tiled=True)
        return out.reshape(n, LANES)

    per_ray = pltpu.VMEM((z.ray_blocks, LANES, LANES), F32)
    compact = pltpu.VMEM((z.compact, LANES), F32)
    indices = pltpu.SMEM((z.slots,), jnp.int32)

    codes = pltpu.SMEM((z.slots + 1,), jnp.int32)

    def middle(back, wide, last):
        scratch = (compact, compact, per_ray, per_ray, codes)
        out = (message, f32(8, LANES))
        return call(
            middle_kernel, "middle2" if last else "middle1", (VMEM,) * 4,
            out if last else out + (wide_rays,), (VMEM,) * (2 if last else 3),
            code, back, wide, tiles_v, scratch=(per_ray,) + scratch if last else scratch,
        )

    msg, wide, code, tiles_v = call(
        first_kernel, "first", [HBM, HBM, SMEM, HBM, HBM],
        (message, wide_rays, jax.ShapeDtypeStruct((z.slots + 8, LANES), jnp.int32), f32(*tiles.shape)),
        (VMEM,) * 4,
        in_hbm(tile_ray), in_hbm(tile_vox), tile_count, in_hbm(travel), in_hbm(tiles),
        scratch=(
            compact, compact, pltpu.VMEM((LANES, LANES), F32), indices, indices,
            pltpu.VMEM(travel.shape, F32), pltpu.SMEM((z.n_vox,), jnp.int32),
            pltpu.SemaphoreType.DMA((z.slots // GROUP,)), pltpu.SemaphoreType.DMA((3,)),
        ),
    )
    n, m = z.data_rows * z.peers, z.segs * VBD
    back, y1, onehot, onehot_t = call(
        owner_first_kernel, "owner1", [VMEM],
        (message, owned, jax.ShapeDtypeStruct((m, n), BF16), jax.ShapeDtypeStruct((n, m), BF16)),
        (VMEM,) * 4, exchange(msg),
    )
    msg, scal1, wide = middle(exchange(back), wide, False)
    back, y2 = call(
        owner_next_kernel, "owner2", [VMEM] * 5, (message, owned), (VMEM,) * 2,
        exchange(msg), onehot, onehot_t, scal1, y1,
    )
    msg, scal2 = middle(exchange(back), wide, True)
    share, back = call(
        owner_last_kernel, "owner3", [VMEM] * 6, (f32(3 * VBD, LANES), f32(z.peers, LANES)),
        (VMEM,) * 2, exchange(msg), onehot, scal1, scal2, y1, y2,
    )
    shares = [share] + [
        lax.ppermute(share, "ray", [(r, r ^ hop) for r in range(n_ray)]) for hop in range(1, n_ray)
    ]
    return call(
        final_kernel, "final", [VMEM] * (1 + n_ray), (owned, owned), (VMEM,) * 2,
        exchange(back), *shares,
    )


def solution(mesh):
    return jax.shard_map(
        on_device,
        mesh=mesh,
        in_specs=(
            P(("ray", "vox"), None, None),
            P(("ray", "vox")),
            P(("ray", "vox")),
            P(("ray", "vox")),
            P(("ray", "vox"), None),
        ),
        out_specs=(P("vox", None), P("vox", None)),
        check_vma=False,
    )
```

```python
import functools

import jax
import jax.numpy as jnp
from jax import lax
from jax.experimental import pallas as pl
from jax.experimental.pallas import tpu as pltpu
from jax.sharding import PartitionSpec as P

VBD = 64
LANES = 128
GROUP = 16
F32 = jnp.float32
BF16 = jnp.bfloat16


class Sizes:
    def __init__(self, n_ray, n_vox, slots, ray_blocks):
        self.n_ray, self.n_vox, self.slots, self.ray_blocks = n_ray, n_vox, slots, ray_blocks
        self.peers = n_ray * n_vox
        self.cap = 2 * slots // n_vox
        self.seg = LANES // n_ray
        self.data_rows = max(1, self.cap * self.seg // LANES)
        self.segs = self.cap // self.data_rows
        self.rows = self.data_rows + 1
        self.compact = self.cap * n_vox


def lane(shape):
    return lax.broadcasted_iota(jnp.int32, shape, len(shape) - 1)


def total(x):
    return jnp.sum(jnp.sum(x, axis=1, keepdims=True), axis=0, keepdims=True)


def pick(row, k):
    return jnp.sum(jnp.where(lane(row.shape) == k, row, 0.0), axis=1, keepdims=True)


def shift_lanes(x, amount):
    amount = amount % LANES
    return x if amount == 0 else pltpu.roll(x, amount, axis=1)


def split3(x):
    hi = x.astype(BF16)
    rest = x - hi.astype(F32)
    mid = rest.astype(BF16)
    low = (rest - mid.astype(F32)).astype(BF16)
    return jnp.concatenate([hi, mid, low], axis=1)


def select_dot(onehot, x):
    width = x.shape[1]
    out = jnp.dot(onehot, split3(x), preferred_element_type=F32)
    return out[:, :width] + out[:, width : 2 * width] + out[:, 2 * width :]


def tile_copy(tiles_hbm, tiles_v, sem, c):
    part = pl.ds(c * GROUP, GROUP)
    return pltpu.make_async_copy(tiles_hbm.at[part], tiles_v.at[part], sem.at[c])


def write_products(z, prod, msg, meta):
    segment = lane((z.n_vox, LANES)) // z.seg
    for q in range(z.data_rows):
        part = [
            prod[pl.ds((q * z.segs + g) * z.n_vox, z.n_vox), :] for g in range(z.segs)
        ]
        for r in range(z.n_ray):
            out = jnp.zeros((z.n_vox, LANES), F32)
            for g in range(z.segs):
                out = jnp.where(segment == g, shift_lanes(part[g], (g - r) * z.seg), out)
            msg[pl.ds(r * z.n_vox * z.rows + q, z.n_vox, stride=z.rows), :] = out
    for r in range(z.n_ray):
        msg[pl.ds(r * z.n_vox * z.rows + z.data_rows, z.n_vox, stride=z.rows), :] = jnp.where(
            lane((z.n_vox, LANES)) == z.cap + 1, jnp.float32(r), meta
        )


def backward(groups, where_of, tiles_v, wide, prod, ready=None):
    def step(c, carry):
        if ready is not None:
            ready(c)
        for s in range(GROUP):
            t = c * GROUP + s
            ray, row = where_of(t)
            prod[pl.ds(row, 1), :] = jnp.sum(tiles_v[t] * wide[ray], axis=0, keepdims=True)
        return carry

    lax.fori_loop(0, groups, step, 0)


def first_kernel(
    z, ray_hbm, vox_hbm, tile_count, travel_hbm, tiles_hbm, msg, wide, code, tiles_v,
    prod, named, pad, tile_ray, tile_vox, travel, count, sem, small_sem,
):
    small = [
        pltpu.make_async_copy(src, dst, small_sem.at[i])
        for i, (src, dst) in enumerate(
            [(travel_hbm, travel), (ray_hbm, tile_ray), (vox_hbm, tile_vox)]
        )
    ]
    live = tile_count[0]
    groups = lax.shift_right_logical(live + (GROUP - 1), GROUP.bit_length() - 1)
    for copy in small:
        copy.start()
    for c in range(z.slots // GROUP):

        @pl.when(c < groups)
        def _():
            tile_copy(tiles_hbm, tiles_v, sem, c).start()

    for o in range(z.n_vox):
        count[o] = 0
    prod[...] = jnp.zeros_like(prod)
    named[...] = jnp.full_like(named, -1.0)
    code[...] = jnp.zeros_like(code)
    pad[...] = jnp.zeros_like(pad)
    small[0].wait()
    pad[pl.ds(0, z.ray_blocks), :] = travel[...]
    by_col = pad[...].T
    for r in range(z.ray_blocks):
        wide[r] = jnp.broadcast_to(by_col[:, r : r + 1], (LANES, LANES))
    for copy in small[1:]:
        copy.wait()

    def ready(c):
        tile_copy(tiles_hbm, tiles_v, sem, c).wait()

    def where_of(t):
        vox, ray = tile_vox[t], tile_ray[t]
        owner = lax.shift_right_logical(vox, VBD.bit_length() - 1)
        k = count[owner]
        count[owner] = k + 1
        row = k * z.n_vox + owner
        code[pl.ds(t, 1), :] = jnp.full((1, LANES), row * 256 + ray, jnp.int32)
        block = jnp.where(t < live, vox & (VBD - 1), -1).astype(F32)
        named[pl.ds(row, 1), :] = jnp.full((1, LANES), block, F32)
        return ray, row

    code[pl.ds(z.slots, 1), :] = jnp.full((1, LANES), groups, jnp.int32)
    backward(groups, where_of, tiles_v, wide, prod, ready)
    here = lane((z.n_vox, LANES))
    meta = jnp.where(here == z.cap, total(travel[...] * travel[...]), 0.0)
    for k in range(z.cap):
        meta = jnp.where(here == k, named[pl.ds(k * z.n_vox, z.n_vox), :], meta)
    write_products(z, prod, msg, meta)


def middle_kernel(
    z, code_v, back, old, tiles_v, msg, scal, *refs
):
    prod, vox_rows, sums, sems, code = refs[-5:]
    wide = refs[0] if len(refs) > 5 else sums
    for t in range(z.slots + 1):
        code[t] = code_v[t, 0]
    meta = back[pl.ds(z.data_rows, z.peers, stride=z.rows), :]
    alpha = jnp.sqrt(pick(jnp.sum(meta, axis=0, keepdims=True), 0))
    beta = pick(meta[0:1], 1)
    here = lane((8, LANES))
    scal[...] = jnp.where(here == 0, alpha, jnp.where(here == 1, beta, 0.0))
    segment = lane((z.n_vox, LANES)) // z.seg
    for q in range(z.data_rows):
        part = [
            back[pl.ds(r * z.n_vox * z.rows + q, z.n_vox, stride=z.rows), :]
            for r in range(z.n_ray)
        ]
        for g in range(z.segs):
            row = jnp.zeros((z.n_vox, LANES), F32)
            for r in range(z.n_ray):
                row = jnp.where(segment == r, shift_lanes(part[r], (r - g) * z.seg), row)
            vox_rows[pl.ds((q * z.segs + g) * z.n_vox, z.n_vox), :] = row / alpha
    lane_share = -alpha / beta * (1.0 / LANES)
    for r in range(z.ray_blocks):
        sums[r] = old[r] * lane_share
        sems[r] = jnp.zeros((LANES, LANES), F32)
    prod[...] = jnp.zeros_like(prod)
    groups = code[z.slots]

    def where_of(t):
        both = code[t]
        return both & 255, lax.shift_right_logical(both, 8)

    def step(c, carry):
        for s in range(GROUP):
            t = c * GROUP + s
            ray, row = where_of(t)
            into = sums if s % 2 == 0 else sems
            into[ray] += tiles_v[t] * vox_rows[pl.ds(row, 1), :]
        return carry

    lax.fori_loop(0, groups, step, 0)
    square = jnp.zeros((LANES, LANES), F32)
    for r in range(z.ray_blocks):
        both = sums[r] + sems[r]
        if r % 4 == 3:
            ones = jnp.ones((3 * LANES, LANES), BF16)
            u = jnp.dot(split3(both), ones, preferred_element_type=F32)
        else:
            u = jnp.broadcast_to(jnp.sum(both, axis=1, keepdims=True), (LANES, LANES))
        wide[r] = u
        square += u * u
    backward(groups, where_of, tiles_v, wide, prod)
    meta = jnp.where(
        lane((z.n_vox, LANES)) == z.cap, total(square) * (1.0 / LANES), 0.0
    )
    write_products(z, prod, msg, meta)


def one_hots(z, meta, onehot, onehot_t):
    wide = jnp.concatenate(
        [shift_lanes(meta, -q * z.segs) for q in range(z.data_rows)], axis=0
    )
    n = z.data_rows * z.peers
    tall = wide.T
    block = lax.broadcasted_iota(jnp.int32, (VBD, n), 0).astype(F32)
    for g in range(z.segs):
        onehot[pl.ds(g * VBD, VBD), :] = (tall[g : g + 1, :] == block).astype(F32).astype(BF16)
    here = lane((n, LANES))
    local = (here % VBD).astype(F32)
    per = LANES // VBD
    for h in range(z.segs // per):
        named = wide[:, h * per : h * per + 1]
        for e in range(1, per):
            named = jnp.where(here // VBD == e, wide[:, h * per + e : h * per + e + 1], named)
        onehot_t[:, pl.ds(h * LANES, LANES)] = (named == local).astype(F32).astype(BF16)


def own_sum(z, msg, onehot):
    data = jnp.concatenate(
        [msg[pl.ds(q, z.peers, stride=z.rows), :] for q in range(z.data_rows)], axis=0
    )
    part = select_dot(onehot[...], data)
    segment = lane((VBD, LANES)) // z.seg
    out = jnp.zeros((VBD, LANES), F32)
    for g in range(z.segs):
        out = jnp.where(segment == g, part[g * VBD : (g + 1) * VBD], out)
    step = LANES // 2
    while step >= z.seg:
        out = out + shift_lanes(out, step)
        step //= 2
    return out


def give_back(z, y, onehot_t, beta, back):
    segment = lane((VBD, LANES)) // z.seg
    square = total(jnp.where(segment == 0, y * y, 0.0))
    spread = jnp.concatenate(
        [jnp.where(segment == g, y, 0.0) for g in range(z.segs)], axis=0
    )
    data = select_dot(onehot_t[...], spread)
    for q in range(z.data_rows):
        back[pl.ds(q, z.peers, stride=z.rows), :] = data[q * z.peers : (q + 1) * z.peers]
    here = lane((z.peers, LANES))
    back[pl.ds(z.data_rows, z.peers, stride=z.rows), :] = jnp.where(
        here == 0, square, jnp.where(here == 1, beta, 0.0)
    )


def message_beta(z, msg):
    meta = msg[pl.ds(z.data_rows, z.peers, stride=z.rows), :]
    return meta, jnp.sqrt(pick(jnp.sum(meta, axis=0, keepdims=True), z.cap))


def owner_first_kernel(z, msg, back, y_out, onehot, onehot_t):
    meta, beta = message_beta(z, msg)
    one_hots(z, meta, onehot, onehot_t)
    y = own_sum(z, msg, onehot) / beta
    y_out[...] = y
    give_back(z, y, onehot_t, beta, back)


def owner_next_kernel(z, msg, onehot, onehot_t, scal, y_in, back, y_out):
    _, beta = message_beta(z, msg)
    alpha = scal[0:1, 0:1]
    y = own_sum(z, msg, onehot) / beta - beta * (y_in[...] / alpha)
    y_out[...] = y
    give_back(z, y, onehot_t, beta, back)


def owner_last_kernel(z, msg, onehot, scal1, scal2, y1, y2, share, back):
    meta, beta3 = message_beta(z, msg)
    mine = pick(meta[0:1], z.cap + 1)
    alpha1, beta1 = scal1[0:1, 0:1], scal1[0:1, 1:2]
    alpha2, beta2 = scal2[0:1, 0:1], scal2[0:1, 1:2]
    v1, v2 = y1[...] / alpha1, y2[...] / alpha2
    w = own_sum(z, msg, onehot) / beta3 - beta3 * v2
    rho1 = jnp.sqrt(alpha1 * alpha1 + beta2 * beta2)
    c1, s1 = alpha1 / rho1, beta2 / rho1
    solution = c1 * beta1 / rho1 * v1
    direction = v2 - s1 * alpha2 / rho1 * v1
    rhobar, phibar = -c1 * alpha2, s1 * beta1
    rho2 = jnp.sqrt(rhobar * rhobar + beta3 * beta3)
    solution = solution + (rhobar / rho2) * phibar / rho2 * direction
    segment = lane((VBD, LANES)) // z.seg
    keep = segment.astype(F32) == mine
    share[pl.ds(0, VBD), :] = jnp.where(keep, w, 0.0)
    share[pl.ds(VBD, VBD), :] = jnp.where(keep, solution, 0.0)
    share[pl.ds(2 * VBD, VBD), :] = jnp.where(keep, direction, 0.0)
    here = lane((z.peers, LANES))
    square = total(jnp.where(segment == 0, w * w, 0.0))
    back[...] = jnp.where(
        here == 0, square, jnp.where(here == 1, beta3 / rho2 / rho2, 0.0)
    )


def final_kernel(z, back, *refs):
    shares, solution, direction = refs[:-2], refs[-2], refs[-1]
    whole = shares[0][...]
    for share in shares[1:]:
        whole = whole + share[...]
    alpha = jnp.sqrt(pick(jnp.sum(back[...], axis=0, keepdims=True), 0))
    factor = pick(back[0:1, :], 1) * alpha
    solution[...] = whole[VBD : 2 * VBD]
    direction[...] = whole[:VBD] / alpha - factor * whole[2 * VBD :]


SMEM = pl.BlockSpec(memory_space=pltpu.SMEM)
VMEM = pl.BlockSpec(memory_space=pltpu.VMEM)
HBM = pl.BlockSpec(memory_space=pltpu.HBM)
PARAMS = pltpu.CompilerParams(vmem_limit_bytes=24 * 1024 * 1024)


def in_hbm(x):
    return pltpu.with_memory_space_constraint(x, pltpu.HBM)


def f32(*shape):
    return jax.ShapeDtypeStruct(shape, F32)


def on_device(tiles, tile_ray, tile_vox, tile_count, travel):
    n_ray, n_vox = lax.axis_size("ray"), lax.axis_size("vox")
    z = Sizes(n_ray, n_vox, tiles.shape[0], travel.shape[0])
    message = f32(z.peers * z.rows, LANES)
    wide_rays = f32(z.ray_blocks, LANES, LANES)
    owned = f32(VBD, LANES)

    def call(kernel, name, in_specs, out_shape, out_specs, *args, scratch=()):
        return pl.pallas_call(
            functools.partial(kernel, z), name=name, in_specs=in_specs, out_shape=out_shape,
            out_specs=out_specs, scratch_shapes=scratch, compiler_params=PARAMS,
        )(*args)

    def exchange(x):
        n = x.shape[0]
        out = lax.all_to_all(x.reshape(n, 1, LANES), ("ray", "vox"), 0, 0, tiled=True)
        return out.reshape(n, LANES)

    per_ray = pltpu.VMEM((z.ray_blocks, LANES, LANES), F32)
    compact = pltpu.VMEM((z.compact, LANES), F32)
    indices = pltpu.SMEM((z.slots,), jnp.int32)

    codes = pltpu.SMEM((z.slots + 1,), jnp.int32)

    def middle(back, wide, last):
        scratch = (compact, compact, per_ray, per_ray, codes)
        out = (message, f32(8, LANES))
        return call(
            middle_kernel, "middle2" if last else "middle1", (VMEM,) * 4,
            out if last else out + (wide_rays,), (VMEM,) * (2 if last else 3),
            code, back, wide, tiles_v, scratch=scratch,
        )

    msg, wide, code, tiles_v = call(
        first_kernel, "first", [HBM, HBM, SMEM, HBM, HBM],
        (message, wide_rays, jax.ShapeDtypeStruct((z.slots + 8, LANES), jnp.int32), f32(*tiles.shape)),
        (VMEM,) * 4,
        in_hbm(tile_ray), in_hbm(tile_vox), tile_count, in_hbm(travel), in_hbm(tiles),
        scratch=(
            compact, compact, pltpu.VMEM((LANES, LANES), F32), indices, indices,
            pltpu.VMEM(travel.shape, F32), pltpu.SMEM((z.n_vox,), jnp.int32),
            pltpu.SemaphoreType.DMA((z.slots // GROUP,)), pltpu.SemaphoreType.DMA((3,)),
        ),
    )
    n, m = z.data_rows * z.peers, z.segs * VBD
    back, y1, onehot, onehot_t = call(
        owner_first_kernel, "owner1", [VMEM],
        (message, owned, jax.ShapeDtypeStruct((m, n), BF16), jax.ShapeDtypeStruct((n, m), BF16)),
        (VMEM,) * 4, exchange(msg),
    )
    msg, scal1, wide = middle(exchange(back), wide, False)
    back, y2 = call(
        owner_next_kernel, "owner2", [VMEM] * 5, (message, owned), (VMEM,) * 2,
        exchange(msg), onehot, onehot_t, scal1, y1,
    )
    msg, scal2 = middle(exchange(back), wide, True)
    share, back = call(
        owner_last_kernel, "owner3", [VMEM] * 6, (f32(3 * VBD, LANES), f32(z.peers, LANES)),
        (VMEM,) * 2, exchange(msg), onehot, scal1, scal2, y1, y2,
    )
    shares = [share] + [
        lax.ppermute(share, "ray", [(r, r ^ hop) for r in range(n_ray)]) for hop in range(1, n_ray)
    ]
    return call(
        final_kernel, "final", [VMEM] * (1 + n_ray), (owned, owned), (VMEM,) * 2,
        exchange(back), *shares,
    )


def solution(mesh):
    return jax.shard_map(
        on_device,
        mesh=mesh,
        in_specs=(
            P(("ray", "vox"), None, None),
            P(("ray", "vox")),
            P(("ray", "vox")),
            P(("ray", "vox")),
            P(("ray", "vox"), None),
        ),
        out_specs=(P("vox", None), P("vox", None)),
        check_vma=False,
    )
```

```python
import functools

import jax
import jax.numpy as jnp
from jax import lax
from jax.experimental import pallas as pl
from jax.experimental.pallas import tpu as pltpu
from jax.sharding import PartitionSpec as P

VBD = 64
LANES = 128
GROUP = 16
F32 = jnp.float32
BF16 = jnp.bfloat16


class Sizes:
    def __init__(self, n_ray, n_vox, slots, ray_blocks):
        self.n_ray, self.n_vox, self.slots, self.ray_blocks = n_ray, n_vox, slots, ray_blocks
        self.peers = n_ray * n_vox
        self.cap = 2 * slots // n_vox
        self.seg = LANES // n_ray
        self.data_rows = max(1, self.cap * self.seg // LANES)
        self.segs = self.cap // self.data_rows
        self.rows = self.data_rows + 1
        self.compact = self.cap * n_vox


def lane(shape):
    return lax.broadcasted_iota(jnp.int32, shape, len(shape) - 1)


def total(x):
    return jnp.sum(jnp.sum(x, axis=1, keepdims=True), axis=0, keepdims=True)


def pick(row, k):
    return jnp.sum(jnp.where(lane(row.shape) == k, row, 0.0), axis=1, keepdims=True)


def shift_lanes(x, amount):
    amount = amount % LANES
    return x if amount == 0 else pltpu.roll(x, amount, axis=1)


def split3(x):
    hi = x.astype(BF16)
    rest = x - hi.astype(F32)
    mid = rest.astype(BF16)
    low = (rest - mid.astype(F32)).astype(BF16)
    return jnp.concatenate([hi, mid, low], axis=1)


def select_dot(onehot, x):
    width = x.shape[1]
    out = jnp.dot(onehot, split3(x), preferred_element_type=F32)
    return out[:, :width] + out[:, width : 2 * width] + out[:, 2 * width :]


def tile_copy(tiles_hbm, tiles_v, sem, c):
    part = pl.ds(c * GROUP, GROUP)
    return pltpu.make_async_copy(tiles_hbm.at[part], tiles_v.at[part], sem.at[c])


def write_products(z, prod, msg, meta):
    segment = lane((z.n_vox, LANES)) // z.seg
    for q in range(z.data_rows):
        part = [
            prod[pl.ds((q * z.segs + g) * z.n_vox, z.n_vox), :] for g in range(z.segs)
        ]
        for r in range(z.n_ray):
            out = jnp.zeros((z.n_vox, LANES), F32)
            for g in range(z.segs):
                out = jnp.where(segment == g, shift_lanes(part[g], (g - r) * z.seg), out)
            msg[pl.ds(r * z.n_vox * z.rows + q, z.n_vox, stride=z.rows), :] = out
    for r in range(z.n_ray):
        msg[pl.ds(r * z.n_vox * z.rows + z.data_rows, z.n_vox, stride=z.rows), :] = jnp.where(
            lane((z.n_vox, LANES)) == z.cap + 1, jnp.float32(r), meta
        )


def backward(groups, where_of, tiles_v, wide, prod, ready=None):
    def step(c, carry):
        if ready is not None:
            ready(c)
        for s in range(GROUP):
            t = c * GROUP + s
            ray, row = where_of(t)
            prod[pl.ds(row, 1), :] = jnp.sum(tiles_v[t] * wide[ray], axis=0, keepdims=True)
        return carry

    lax.fori_loop(0, groups, step, 0)


def first_kernel(
    z, ray_hbm, vox_hbm, tile_count, travel_hbm, tiles_hbm, msg, wide, code, tiles_v,
    prod, named, pad, tile_ray, tile_vox, travel, count, sem, small_sem,
):
    small = [
        pltpu.make_async_copy(src, dst, small_sem.at[i])
        for i, (src, dst) in enumerate(
            [(travel_hbm, travel), (ray_hbm, tile_ray), (vox_hbm, tile_vox)]
        )
    ]
    live = tile_count[0]
    groups = lax.shift_right_logical(live + (GROUP - 1), GROUP.bit_length() - 1)
    for copy in small:
        copy.start()
    for c in range(z.slots // GROUP):

        @pl.when(c < groups)
        def _():
            tile_copy(tiles_hbm, tiles_v, sem, c).start()

    for o in range(z.n_vox):
        count[o] = 0
    prod[...] = jnp.zeros_like(prod)
    named[...] = jnp.full_like(named, -1.0)
    code[...] = jnp.zeros_like(code)
    pad[...] = jnp.zeros_like(pad)
    small[0].wait()
    pad[pl.ds(0, z.ray_blocks), :] = travel[...]
    by_col = pad[...].T
    for r in range(z.ray_blocks):
        wide[r] = jnp.broadcast_to(by_col[:, r : r + 1], (LANES, LANES))
    square = total(travel[...] * travel[...])
    for copy in small[1:]:
        copy.wait()

    def ready(c):
        tile_copy(tiles_hbm, tiles_v, sem, c).wait()

    def where_of(t):
        vox, ray = tile_vox[t], tile_ray[t]
        owner = lax.shift_right_logical(vox, VBD.bit_length() - 1)
        k = count[owner]
        count[owner] = k + 1
        row = k * z.n_vox + owner
        code[pl.ds(t, 1), :] = jnp.full((1, LANES), row * 256 + ray, jnp.int32)
        block = jnp.where(t < live, vox & (VBD - 1), -1).astype(F32)
        named[pl.ds(row, 1), :] = jnp.full((1, LANES), block, F32)
        return ray, row

    code[pl.ds(z.slots, 1), :] = jnp.full((1, LANES), groups, jnp.int32)
    backward(groups, where_of, tiles_v, wide, prod, ready)
    here = lane((z.n_vox, LANES))
    meta = jnp.where(here == z.cap, square, 0.0)
    for k in range(z.cap):
        meta = jnp.where(here == k, named[pl.ds(k * z.n_vox, z.n_vox), :], meta)
    write_products(z, prod, msg, meta)


def middle_kernel(
    z, code_v, back, old, tiles_v, msg, scal, *refs
):
    wide, prod, vox_rows, sums, sems, code = refs
    for t in range(z.slots + 1):
        code[t] = code_v[t, 0]
    meta = back[pl.ds(z.data_rows, z.peers, stride=z.rows), :]
    alpha = jnp.sqrt(pick(jnp.sum(meta, axis=0, keepdims=True), 0))
    beta = pick(meta[0:1], 1)
    here = lane((8, LANES))
    scal[...] = jnp.where(here == 0, alpha, jnp.where(here == 1, beta, 0.0))
    segment = lane((z.n_vox, LANES)) // z.seg
    for q in range(z.data_rows):
        part = [
            back[pl.ds(r * z.n_vox * z.rows + q, z.n_vox, stride=z.rows), :]
            for r in range(z.n_ray)
        ]
        for g in range(z.segs):
            row = jnp.zeros((z.n_vox, LANES), F32)
            for r in range(z.n_ray):
                row = jnp.where(segment == r, shift_lanes(part[r], (r - g) * z.seg), row)
            vox_rows[pl.ds((q * z.segs + g) * z.n_vox, z.n_vox), :] = row / alpha
    lane_share = -alpha / beta * (1.0 / LANES)
    for r in range(z.ray_blocks):
        sums[r] = old[r] * lane_share
        sems[r] = jnp.zeros((LANES, LANES), F32)
    prod[...] = jnp.zeros_like(prod)
    groups = code[z.slots]

    def where_of(t):
        both = code[t]
        return both & 255, lax.shift_right_logical(both, 8)

    def step(c, carry):
        for s in range(GROUP):
            t = c * GROUP + s
            ray, row = where_of(t)
            into = sums if s % 2 == 0 else sems
            into[ray] += tiles_v[t] * vox_rows[pl.ds(row, 1), :]
        return carry

    lax.fori_loop(0, groups, step, 0)
    square = jnp.zeros((LANES, LANES), F32)
    for r in range(z.ray_blocks):
        u = jnp.broadcast_to(
            jnp.sum(sums[r] + sems[r], axis=1, keepdims=True), (LANES, LANES)
        )
        wide[r] = u
        square += u * u
    backward(groups, where_of, tiles_v, wide, prod)
    meta = jnp.where(
        lane((z.n_vox, LANES)) == z.cap, total(square) * (1.0 / LANES), 0.0
    )
    write_products(z, prod, msg, meta)


def one_hots(z, meta, onehot, onehot_t):
    wide = jnp.concatenate(
        [shift_lanes(meta, -q * z.segs) for q in range(z.data_rows)], axis=0
    )
    n = z.data_rows * z.peers
    tall = wide.T
    block = lax.broadcasted_iota(jnp.int32, (VBD, n), 0).astype(F32)
    for g in range(z.segs):
        onehot[pl.ds(g * VBD, VBD), :] = (tall[g : g + 1, :] == block).astype(F32).astype(BF16)
    here = lane((n, LANES))
    local = (here % VBD).astype(F32)
    per = LANES // VBD
    for h in range(z.segs // per):
        named = wide[:, h * per : h * per + 1]
        for e in range(1, per):
            named = jnp.where(here // VBD == e, wide[:, h * per + e : h * per + e + 1], named)
        onehot_t[:, pl.ds(h * LANES, LANES)] = (named == local).astype(F32).astype(BF16)


def own_sum(z, msg, onehot):
    data = jnp.concatenate(
        [msg[pl.ds(q, z.peers, stride=z.rows), :] for q in range(z.data_rows)], axis=0
    )
    part = select_dot(onehot[...], data)
    segment = lane((VBD, LANES)) // z.seg
    out = jnp.zeros((VBD, LANES), F32)
    for g in range(z.segs):
        out = jnp.where(segment == g, part[g * VBD : (g + 1) * VBD], out)
    step = LANES // 2
    while step >= z.seg:
        out = out + shift_lanes(out, step)
        step //= 2
    return out


def give_back(z, y, onehot_t, beta, back):
    segment = lane((VBD, LANES)) // z.seg
    square = total(jnp.where(segment == 0, y * y, 0.0))
    spread = jnp.concatenate(
        [jnp.where(segment == g, y, 0.0) for g in range(z.segs)], axis=0
    )
    data = select_dot(onehot_t[...], spread)
    for q in range(z.data_rows):
        back[pl.ds(q, z.peers, stride=z.rows), :] = data[q * z.peers : (q + 1) * z.peers]
    here = lane((z.peers, LANES))
    back[pl.ds(z.data_rows, z.peers, stride=z.rows), :] = jnp.where(
        here == 0, square, jnp.where(here == 1, beta, 0.0)
    )


def message_beta(z, msg):
    meta = msg[pl.ds(z.data_rows, z.peers, stride=z.rows), :]
    return meta, jnp.sqrt(pick(jnp.sum(meta, axis=0, keepdims=True), z.cap))


def owner_first_kernel(z, msg, back, y_out, onehot, onehot_t):
    meta, beta = message_beta(z, msg)
    one_hots(z, meta, onehot, onehot_t)
    y = own_sum(z, msg, onehot) / beta
    y_out[...] = y
    give_back(z, y, onehot_t, beta, back)


def owner_next_kernel(z, msg, onehot, onehot_t, scal, y_in, back, y_out):
    _, beta = message_beta(z, msg)
    alpha = scal[0:1, 0:1]
    y = own_sum(z, msg, onehot) / beta - beta * (y_in[...] / alpha)
    y_out[...] = y
    give_back(z, y, onehot_t, beta, back)


def owner_last_kernel(z, msg, onehot, scal1, scal2, y1, y2, share, back):
    meta, beta3 = message_beta(z, msg)
    mine = pick(meta[0:1], z.cap + 1)
    alpha1, beta1 = scal1[0:1, 0:1], scal1[0:1, 1:2]
    alpha2, beta2 = scal2[0:1, 0:1], scal2[0:1, 1:2]
    v1, v2 = y1[...] / alpha1, y2[...] / alpha2
    w = own_sum(z, msg, onehot) / beta3 - beta3 * v2
    rho1 = jnp.sqrt(alpha1 * alpha1 + beta2 * beta2)
    c1, s1 = alpha1 / rho1, beta2 / rho1
    solution = c1 * beta1 / rho1 * v1
    direction = v2 - s1 * alpha2 / rho1 * v1
    rhobar, phibar = -c1 * alpha2, s1 * beta1
    rho2 = jnp.sqrt(rhobar * rhobar + beta3 * beta3)
    solution = solution + (rhobar / rho2) * phibar / rho2 * direction
    segment = lane((VBD, LANES)) // z.seg
    keep = segment.astype(F32) == mine
    share[pl.ds(0, VBD), :] = jnp.where(keep, w, 0.0)
    share[pl.ds(VBD, VBD), :] = jnp.where(keep, solution, 0.0)
    share[pl.ds(2 * VBD, VBD), :] = jnp.where(keep, direction, 0.0)
    here = lane((z.peers, LANES))
    square = total(jnp.where(segment == 0, w * w, 0.0))
    back[...] = jnp.where(
        here == 0, square, jnp.where(here == 1, beta3 / rho2 / rho2, 0.0)
    )


def final_kernel(z, back, *refs):
    shares, solution, direction = refs[:-2], refs[-2], refs[-1]
    whole = shares[0][...]
    for share in shares[1:]:
        whole = whole + share[...]
    alpha = jnp.sqrt(pick(jnp.sum(back[...], axis=0, keepdims=True), 0))
    factor = pick(back[0:1, :], 1) * alpha
    solution[...] = whole[VBD : 2 * VBD]
    direction[...] = whole[:VBD] / alpha - factor * whole[2 * VBD :]


SMEM = pl.BlockSpec(memory_space=pltpu.SMEM)
VMEM = pl.BlockSpec(memory_space=pltpu.VMEM)
HBM = pl.BlockSpec(memory_space=pltpu.HBM)
PARAMS = pltpu.CompilerParams(vmem_limit_bytes=24 * 1024 * 1024)


def in_hbm(x):
    return pltpu.with_memory_space_constraint(x, pltpu.HBM)


def f32(*shape):
    return jax.ShapeDtypeStruct(shape, F32)


def on_device(tiles, tile_ray, tile_vox, tile_count, travel):
    n_ray, n_vox = lax.axis_size("ray"), lax.axis_size("vox")
    z = Sizes(n_ray, n_vox, tiles.shape[0], travel.shape[0])
    message = f32(z.peers * z.rows, LANES)
    wide_rays = f32(z.ray_blocks, LANES, LANES)
    owned = f32(VBD, LANES)

    def call(kernel, name, in_specs, out_shape, out_specs, *args, scratch=()):
        return pl.pallas_call(
            functools.partial(kernel, z), name=name, in_specs=in_specs, out_shape=out_shape,
            out_specs=out_specs, scratch_shapes=scratch, compiler_params=PARAMS,
        )(*args)

    def exchange(x):
        n = x.shape[0]
        out = lax.all_to_all(x.reshape(n, 1, LANES), ("ray", "vox"), 0, 0, tiled=True)
        return out.reshape(n, LANES)

    per_ray = pltpu.VMEM((z.ray_blocks, LANES, LANES), F32)
    compact = pltpu.VMEM((z.compact, LANES), F32)
    indices = pltpu.SMEM((z.slots,), jnp.int32)

    codes = pltpu.SMEM((z.slots + 1,), jnp.int32)

    def middle(back, wide, last):
        scratch = (compact, compact, per_ray, per_ray, codes)
        out = (message, f32(8, LANES))
        return call(
            middle_kernel, "middle2" if last else "middle1", (VMEM,) * 4,
            out if last else out + (wide_rays,), (VMEM,) * (2 if last else 3),
            code, back, wide, tiles_v, scratch=(per_ray,) + scratch if last else scratch,
        )

    msg, wide, code, tiles_v = call(
        first_kernel, "first", [HBM, HBM, SMEM, HBM, HBM],
        (message, wide_rays, jax.ShapeDtypeStruct((z.slots + 8, LANES), jnp.int32), f32(*tiles.shape)),
        (VMEM,) * 4,
        in_hbm(tile_ray), in_hbm(tile_vox), tile_count, in_hbm(travel), in_hbm(tiles),
        scratch=(
            compact, compact, pltpu.VMEM((LANES, LANES), F32), indices, indices,
            pltpu.VMEM(travel.shape, F32), pltpu.SMEM((z.n_vox,), jnp.int32),
            pltpu.SemaphoreType.DMA((z.slots // GROUP,)), pltpu.SemaphoreType.DMA((3,)),
        ),
    )
    n, m = z.data_rows * z.peers, z.segs * VBD
    back, y1, onehot, onehot_t = call(
        owner_first_kernel, "owner1", [VMEM],
        (message, owned, jax.ShapeDtypeStruct((m, n), BF16), jax.ShapeDtypeStruct((n, m), BF16)),
        (VMEM,) * 4, exchange(msg),
    )
    msg, scal1, wide = middle(exchange(back), wide, False)
    back, y2 = call(
        owner_next_kernel, "owner2", [VMEM] * 5, (message, owned), (VMEM,) * 2,
        exchange(msg), onehot, onehot_t, scal1, y1,
    )
    msg, scal2 = middle(exchange(back), wide, True)
    share, back = call(
        owner_last_kernel, "owner3", [VMEM] * 6, (f32(3 * VBD, LANES), f32(z.peers, LANES)),
        (VMEM,) * 2, exchange(msg), onehot, scal1, scal2, y1, y2,
    )
    shares = [share] + [
        lax.ppermute(share, "ray", [(r, r ^ hop) for r in range(n_ray)]) for hop in range(1, n_ray)
    ]
    return call(
        final_kernel, "final", [VMEM] * (1 + n_ray), (owned, owned), (VMEM,) * 2,
        exchange(back), *shares,
    )


def solution(mesh):
    return jax.shard_map(
        on_device,
        mesh=mesh,
        in_specs=(
            P(("ray", "vox"), None, None),
            P(("ray", "vox")),
            P(("ray", "vox")),
            P(("ray", "vox")),
            P(("ray", "vox"), None),
        ),
        out_specs=(P("vox", None), P("vox", None)),
        check_vma=False,
    )
```
